256 devices in a mesh: dp: 16 (over x, y), latent: 16 (over z, core).
Axes of the slice: x: 4, y: 4, z: 8, core: 2. Of those that a mesh axis runs over, the one named last changes fastest.
Arguments:
- queries: bfloat16 [8192, 2048], P(('dp', 'latent')), may hold values from -32 to 32, as said below
- cache_keys: bfloat16 [256, 512, 1024], P(('dp', 'latent')), may hold values from -6 to 6
- cache_values: bfloat16 [256, 512, 1024], P(('dp', 'latent')), may hold values from -96 to 96
- positions: int32 [8192], P(('dp', 'latent')), may hold values from 224 to 511, as said below
- shuffle: int32 [8192], P(('dp', 'latent')), may hold values from 0 to 8191, as said below
- enc_weight: bfloat16 [2048, 16384], P(None, 'latent'), may hold values from -0.125 to 0.125
- enc_bias: float32 [16384], P('latent'), may hold values from -3 to 3
- dec_weight: bfloat16 [16384, 2048], P('latent'), may hold values from -0.046875 to 0.046875
- dec_bias: float32 [2048], replicated, may hold values from -3 to 3
Outputs:
- rebuilt: bfloat16 [8192, 2048], P(('dp', 'latent'))
- grad_enc: float32 [2048, 16384], P('dp', 'latent')
- grad_dec: float32 [16384, 2048], P('latent', 'dp')
The draws below stay inside these ranges and needn't reach their ends.
Inputs may be any that keep to these rules, and one draw needn't show every extreme that they name: `queries`: entries are finite; a few rows may be aligned with keys of their sequence. The rows of one sequence have consecutive positions ending at its length minus one; lengths lie between 256 and 512, and sequence 0 has length 512. A permutation of 0 to 8191. Row r and its place shuffle[r] lie in sequences r // 32 and shuffle[r] // 32 that are equal modulo 512 // 32; from each such sequence exactly 2 rows go to each such sequence.
All inputs are finite; a program needn't handle non-finite values.
Results may differ from the reference program's by a relative error of at most 0.012.
Values may be sent and summed in bfloat16 or wider, within the bound.
A program may use at most 128 MiB of HBM per device.

```python
import math
import jax
import jax.numpy as jnp
from jax import lax

HEADS = 8
KV_HEADS = 4
HEAD_DIM = 256
LATENTS = 16384
Q_DEV = 32
CACHE = 512
D_ATT = 2048
SEQS = 256
ROWS = 8192
GROUP_ROWS = 512
PER_PEER = 2
N_DP = 16
N_LATENT = 16


def attention_draw(key):
    key_part = jax.random.fold_in(key, 101)
    query_part = jax.random.fold_in(key, 102)
    keys_arr = jnp.clip(jax.random.normal(key_part, (SEQS, CACHE, KV_HEADS * HEAD_DIM), jnp.float32), -6.0, 6.0)
    query_arr = jnp.clip(jax.random.normal(query_part, (ROWS, HEADS * HEAD_DIM), jnp.float32), -6.0, 6.0)
    return (query_arr, keys_arr)


def draw_queries(key, part):
    return attention_draw(key)[0].astype(jnp.bfloat16)


def draw_cache_keys(key, part):
    return attention_draw(key)[1].astype(jnp.bfloat16)


def draw_cache_values(key, part):
    value_part = jax.random.fold_in(key, 201)
    slot_part = jax.random.fold_in(key, 202)
    shape = (SEQS, CACHE, KV_HEADS * HEAD_DIM)
    seq_scale = 3.0 ** (jnp.arange(SEQS, dtype=jnp.float32) / max(SEQS - 1, 1))
    slot_scale = jnp.exp(jax.random.uniform(slot_part, (SEQS, CACHE, 1), jnp.float32, math.log(0.5), math.log(5.0)))
    base = jnp.clip(jax.random.normal(value_part, shape, jnp.float32), -6.0, 6.0)
    return (base * slot_scale * seq_scale[:, None, None]).astype(jnp.bfloat16)


def draw_positions(key, part):
    length_part = jax.random.fold_in(key, 301)
    lengths = jax.random.randint(length_part, (SEQS,), CACHE // 2, CACHE + 1)
    lengths = lengths.at[0].set(CACHE)
    offsets = jnp.arange(Q_DEV, dtype=jnp.int32)
    return (lengths[:, None] - Q_DEV + offsets[None, :]).reshape(ROWS).astype(jnp.int32)


def one_permutation(subkey):
    return jax.random.permutation(subkey, Q_DEV)


def draw_shuffle(key, part):
    rank_part = jax.random.fold_in(key, 401)
    place_part = jax.random.fold_in(key, 402)
    ranks = jax.vmap(one_permutation)(jax.random.split(rank_part, SEQS)).astype(jnp.int32)
    places = jax.vmap(one_permutation)(jax.random.split(place_part, SEQS)).astype(jnp.int32)
    device = jnp.arange(SEQS, dtype=jnp.int32)[:, None]
    source_dp = device // N_LATENT
    latent_index = device % N_LATENT
    target_dp = ranks // PER_PEER
    arrival = source_dp * PER_PEER + ranks % PER_PEER
    target_dev = target_dp * N_LATENT + latent_index
    slot = places[target_dev, arrival]
    return (target_dev * Q_DEV + slot).reshape(ROWS).astype(jnp.int32)


def level_of(key, extent, cuts, smallest, high):
    loudness, own = 1.0, jax.random.fold_in(key, 6)
    for axis_at, parts in cuts:
        heights = jnp.exp(jax.random.uniform(jax.random.fold_in(own, axis_at), (parts,), jnp.float32, smallest / len(cuts), high / len(cuts)))
        loudness = loudness * jnp.repeat(heights, extent[axis_at] // parts).reshape([-1 if axis == axis_at else 1 for axis in range(len(extent))])
    return loudness


def bell_draw(rng, shape, scale, bound, pieces=(), kind=jnp.bfloat16):
    drawn = scale * jax.random.normal(rng, shape, jnp.float32)
    if pieces:
        drawn = drawn * level_of(rng, shape, pieces, -0.22, 0.18)
    return jnp.clip(drawn, -bound, bound).astype(kind)


def setup_inputs(seed: int = 0) -> dict:
    key_of = jax.random.split(jax.random.key(seed), 10)
    return {
        "queries": draw_queries(jax.random.fold_in(key_of[9], 71), 0),
        "cache_keys": draw_cache_keys(jax.random.fold_in(key_of[9], 71), 0),
        "cache_values": draw_cache_values(jax.random.fold_in(key_of[9], 71), 0),
        "positions": draw_positions(jax.random.fold_in(key_of[9], 71), 0),
        "shuffle": draw_shuffle(jax.random.fold_in(key_of[9], 71), 0),
        "enc_weight": bell_draw(key_of[5], (D_ATT, LATENTS), D_ATT ** -0.5, 0.125, ((1, 16),)),
        "enc_bias": bell_draw(key_of[6], (LATENTS,), 0.5, 3.0, ((0, 16),), jnp.float32),
        "dec_weight": bell_draw(key_of[7], (LATENTS, D_ATT), LATENTS ** -0.5, 0.046875, ((0, 16),)),
        "dec_bias": bell_draw(key_of[8], (D_ATT,), 0.5, 3.0, (), jnp.float32),
    }


sharpness = 4.0
sparsity_weight = 1.0
epsilon = 1e-06

def attend(query_rows, key_rows, value_rows, position_rows):
    grouped = query_rows.reshape(Q_DEV, KV_HEADS, HEADS // KV_HEADS, HEAD_DIM).astype(jnp.float32)
    keys_local = key_rows.reshape(CACHE, KV_HEADS, HEAD_DIM).astype(jnp.float32)
    values_local = value_rows.reshape(CACHE, KV_HEADS, HEAD_DIM).astype(jnp.float32)
    scores = jnp.einsum('qgid,kgd->gqik', grouped, keys_local) * HEAD_DIM ** (-0.5)
    slot_index = jnp.arange(CACHE)
    visible = slot_index[None, None, None, :] <= position_rows[None, :, None, None]
    scores = jnp.where(visible, scores, -jnp.inf)
    highest = lax.optimization_barrier(jnp.max(scores, axis=-1, keepdims=True))
    weights = jnp.exp(scores - highest)
    weights = weights / lax.optimization_barrier(jnp.sum(weights, axis=-1, keepdims=True))
    attn_probs = lax.optimization_barrier(weights.astype(jnp.bfloat16)).astype(jnp.float32)
    head_mix = jnp.einsum('gqik,kgd->qgid', attn_probs, values_local)
    return head_mix.reshape(Q_DEV, D_ATT).astype(jnp.bfloat16)

def attend_packed(packed):
    return attend(packed[0], packed[1], packed[2], packed[3])

def reference(queries, cache_keys, cache_values, positions, shuffle, enc_weight, enc_bias, dec_weight, dec_bias):
    heads_out = lax.map(attend_packed, (queries.reshape(SEQS, Q_DEV, D_ATT), cache_keys, cache_values, positions.reshape(SEQS, Q_DEV)))
    heads_out = heads_out.reshape(ROWS, D_ATT).astype(jnp.float32)
    energy = jnp.sum(jnp.square(heads_out))
    norm_scale = 1.0 / jnp.sqrt(energy / (ROWS * D_ATT) + epsilon)
    normed = (heads_out * norm_scale).astype(jnp.bfloat16)
    inputs = jnp.zeros_like(normed).at[shuffle].set(normed)
    groups = inputs.reshape(N_DP, GROUP_ROWS, D_ATT)
    dec_float = dec_weight.astype(jnp.float32)
    dec_norms = jnp.sqrt(lax.optimization_barrier(jnp.sum(jnp.square(dec_float), axis=1)) + epsilon)

    def process_group(carry, gathered):
        enc_acc, dec_acc = carry
        preact = jnp.dot(gathered, enc_weight, preferred_element_type=jnp.float32) + enc_bias
        active = jax.nn.softplus(sharpness * preact) / sharpness
        coded = active.astype(jnp.bfloat16)
        rebuilt_full = jnp.dot(coded, dec_weight, preferred_element_type=jnp.float32) + dec_bias
        residual = rebuilt_full - gathered.astype(jnp.float32)
        residual_half = residual.astype(jnp.bfloat16)
        grad_active = 2.0 / ROWS * lax.dot_general(residual_half, dec_weight, (((1,), (1,)), ((), ())), preferred_element_type=jnp.float32)
        grad_active = grad_active + sparsity_weight / ROWS * dec_norms[None, :]
        grad_pre = (grad_active * jax.nn.sigmoid(sharpness * preact)).astype(jnp.bfloat16)
        enc_term = lax.dot_general(gathered, grad_pre, (((0,), (0,)), ((), ())), preferred_element_type=jnp.float32)
        column_sums = lax.optimization_barrier(jnp.sum(coded.astype(jnp.float32), axis=0))
        dec_term = 2.0 / ROWS * lax.dot_general(coded, residual_half, (((0,), (0,)), ((), ())), preferred_element_type=jnp.float32)
        dec_term = dec_term + sparsity_weight / ROWS * column_sums[:, None] * dec_float / dec_norms[:, None]
        enc_acc = enc_acc + enc_term.astype(jnp.bfloat16).astype(jnp.float32)
        dec_acc = dec_acc + dec_term.astype(jnp.bfloat16).astype(jnp.float32)
        return ((enc_acc, dec_acc), rebuilt_full.astype(jnp.bfloat16))
    start_carry = (jnp.zeros((D_ATT, LATENTS), jnp.float32), jnp.zeros((LATENTS, D_ATT), jnp.float32))
    final_carry, rebuilt = lax.scan(process_group, start_carry, groups)
    grad_enc, grad_dec = final_carry
    return (rebuilt.reshape(ROWS, D_ATT), grad_enc, grad_dec)
```

```python
import jax
import jax.numpy as jnp
from jax import lax
from jax.experimental import pallas as pl
from jax.experimental.pallas import tpu as pltpu
from jax.sharding import PartitionSpec as P

F32 = jnp.float32
BF16 = jnp.bfloat16
MESH = pl.DeviceIdType.MESH

HEAD_DIM = 256
KV_HEADS = 4
HEADS = 8
CACHE = 512
ROWS_DEV = 32
GROUP = 512
WIDTH = 2048
LAT = 1024
ALL_ROWS = 8192
N_X = 4
N_Z = 8
N_DP = 16
CHUNKS = 4
COLS = WIDTH // CHUNKS
EPSILON = 1e-06
GRAD_SCALE = 2.0 / ALL_ROWS
SPARSE_SCALE = 1.0 / ALL_ROWS

N_SEMS = 264


def dot(a, b):
    return jnp.dot(a, b, preferred_element_type=F32)


def dot_nt(a, b):
    return lax.dot_general(a, b, (((1,), (1,)), ((), ())), preferred_element_type=F32)


def iota(shape, axis):
    return lax.broadcasted_iota(jnp.int32, shape, axis)


def chunk_dp(j, s):
    return s * N_X + (j - s) % N_X


def kernel(
    queries, keys, values, positions, shuffle, enc_w, enc_bias, dec_w, dec_bias,
    rebuilt_out, enc_out, dec_out,
    q_v, k_v, v_v, enc_v, dec_v, heads, outgoing, arrived, notes_out, notes_in,
    energies, gathered, inputs, batch, inputs_t, coded, coded_t, gate, norm_row, dec_coef,
    part_send, part_recv, part_own, rs_send_p, rs_recv_p, rs_send_m, rs_recv_m,
    residual, grad_act, grad_pre, dec_term, enc_term,
    dec_r1, dec_r2, enc_r1, enc_r2, dec_u, enc_u, dec_s1, dec_s2, enc_s1, enc_s2,
    send_sems, recv_sems, local_sems,
):
    me_dp = lax.axis_index("dp")
    me_l = lax.axis_index("latent")
    x, y = me_dp // N_X, me_dp % N_X
    z, core = me_l // 2, me_l % 2
    other = 1 - core

    def at_z(k):
        return {"latent": lax.rem(z + k + N_Z, N_Z) * 2 + core}

    partner = {"latent": z * 2 + other}

    def at_x(k):
        return {"dp": lax.rem(x + k + N_X, N_X) * N_X + y}

    def at_y(k):
        return {"dp": x * N_X + lax.rem(y + k + N_X, N_X)}

    counter = [0]
    sent = []

    def remote(src, dst, device):
        i = counter[0]
        counter[0] += 1
        return pltpu.make_async_remote_copy(
            src_ref=src, dst_ref=dst, send_sem=send_sems.at[i], recv_sem=recv_sems.at[i],
            device_id=device, device_id_type=MESH,
        )

    def start(copy):
        copy.start()
        sent.append(copy)
        return copy

    def load(src, dst, i):
        c = pltpu.make_async_copy(src, dst, local_sems.at[i])
        c.start()
        return c

    load_q = load(queries, q_v, 0)
    load_k = load(keys.at[0], k_v, 1)
    load_v = load(values.at[0], v_v, 2)
    load_e = load(enc_w, enc_v, 3)
    load_d = []
    for j in range(CHUNKS):
        for s in range(N_X):
            d = chunk_dp(j, s)
            load_d.append(
                load(dec_w.at[:, d * 128:(d + 1) * 128], dec_v.at[j, :, s * 128:(s + 1) * 128], 4 + j * N_X + s)
            )

    barrier = pltpu.get_barrier_semaphore()
    for o in range(1, N_DP):
        pl.semaphore_signal(barrier, inc=1, device_id={"dp": lax.rem(me_dp + o, N_DP)}, device_id_type=MESH)
        pl.semaphore_signal(barrier, inc=1, device_id={"latent": lax.rem(me_l + o, N_DP)}, device_id_type=MESH)

    shuffle_row = shuffle[...]
    sub = iota((ROWS_DEV, ROWS_DEV), 0)
    lane = iota((ROWS_DEV, ROWS_DEV), 1)
    eye = sub == lane
    wide = jnp.broadcast_to(shuffle_row, (ROWS_DEV, ROWS_DEV))
    shuffle_col = jnp.sum(jnp.where(eye, wide.astype(F32), 0.0), axis=1, keepdims=True).astype(jnp.int32)
    target_row = lax.shift_right_logical(wide, 9)
    target_col = lax.shift_right_logical(shuffle_col, 9)
    before = jnp.where((target_row == target_col) & (lane < sub), 1.0, 0.0)
    slot_col = 2.0 * target_col.astype(F32) + jnp.sum(before, axis=1, keepdims=True)
    lane_w = iota((ROWS_DEV, 256), 1)
    sub_w = iota((ROWS_DEV, 256), 0)
    slot_wide = jnp.sum(
        jnp.where((lane_w & 31) == sub_w, jnp.broadcast_to(slot_col, (ROWS_DEV, 256)), 0.0), axis=0, keepdims=True
    ).astype(jnp.int32)
    slot_row = jnp.sum(jnp.where(eye, jnp.broadcast_to(slot_col, (ROWS_DEV, ROWS_DEV)), 0.0), axis=0, keepdims=True)
    slot_row = slot_row.astype(jnp.int32)
    place_row = (shuffle_row & 31).astype(F32)
    sub_q = iota((256, 256), 0)
    lane_q = iota((256, 256), 1)
    pick = (sub_q & 7) == lax.shift_right_logical(lane_q, 5)
    pick = pick & (lax.shift_right_logical(sub_q, 3) == slot_wide)
    pick = jnp.where(pick, 1.0, 0.0).astype(BF16)

    pos_wide = jnp.broadcast_to(positions[...], (ROWS_DEV, ROWS_DEV)).astype(F32)
    pos_col = jnp.sum(jnp.where(eye, pos_wide, 0.0), axis=1, keepdims=True).astype(jnp.int32)
    pos_col = jnp.concatenate([pos_col, pos_col], axis=0)
    visible = iota((2 * ROWS_DEV, CACHE), 1) <= pos_col
    load_q.wait()
    load_k.wait()
    load_v.wait()
    energy = jnp.zeros((1, 1), F32)
    for g in range(KV_HEADS):
        cols = slice(g * HEAD_DIM, (g + 1) * HEAD_DIM)
        pair = jnp.concatenate(
            [q_v[:, (2 * g + i) * HEAD_DIM:(2 * g + i + 1) * HEAD_DIM] for i in range(2)], axis=0
        )
        scores = dot_nt(pair, k_v[:, cols]) * HEAD_DIM ** (-0.5)
        scores = jnp.where(visible, scores, -jnp.inf)
        weights = jnp.exp(scores - jnp.max(scores, axis=1, keepdims=True))
        probs = (weights / jnp.sum(weights, axis=1, keepdims=True)).astype(BF16)
        mixed = dot(probs, v_v[:, cols]).astype(BF16)
        heads[g * 64:(g + 1) * 64, :] = mixed
        square = jnp.square(mixed.astype(F32))
        energy = energy + jnp.sum(jnp.sum(square, axis=1, keepdims=True), axis=0, keepdims=True)
    outgoing[...] = dot(pick, heads[...]).astype(BF16)

    note_sub = iota((128, 256), 0)
    note_lane = iota((128, 256), 1)
    peer_sub = lax.shift_right_logical(iota((128, ROWS_DEV), 0), 3)
    slot_n = jnp.broadcast_to(slot_row, (128, ROWS_DEV))
    place_n = jnp.broadcast_to(place_row, (128, ROWS_DEV))
    place = [
        jnp.sum(jnp.where(slot_n == 2 * peer_sub + k, place_n, 0.0), axis=1, keepdims=True) for k in range(2)
    ]
    mine = lax.shift_right_logical(note_lane, 4) == me_dp
    place_note = jnp.where((lax.shift_right_logical(note_lane, 3) & 1) == 0, place[0], place[1])
    place_note = jnp.where(mine, place_note, 0.0)
    notes_out[...] = jnp.where((note_sub & 7) == 0, place_note, jnp.broadcast_to(energy, (128, 256)))

    pl.semaphore_wait(barrier, 2 * (N_DP - 1))
    own16 = pl.ds(pl.multiple_of(me_dp * 16, 16), 16)
    own8 = pl.ds(pl.multiple_of(me_dp * 8, 8), 8)
    waits = []
    for o in range(1, N_DP):
        to = lax.rem(me_dp + o, N_DP)
        frm = lax.rem(me_dp + N_DP - o, N_DP)
        to16 = pl.ds(pl.multiple_of(to * 16, 16), 16)
        to8 = pl.ds(pl.multiple_of(to * 8, 8), 8)
        frm16 = pl.ds(pl.multiple_of(frm * 16, 16), 16)
        frm8 = pl.ds(pl.multiple_of(frm * 8, 8), 8)
        for src, dst, to_at, own_at, frm_at in (
            (outgoing, arrived, to16, own16, frm16),
            (notes_out, notes_in, to8, own8, frm8),
        ):
            i = counter[0]
            c = start(remote(src.at[to_at], dst.at[own_at], {"dp": to}))
            waits.append(
                pltpu.make_async_remote_copy(
                    src_ref=src.at[to_at], dst_ref=dst.at[frm_at], send_sem=send_sems.at[i],
                    recv_sem=recv_sems.at[i], device_id={"dp": to}, device_id_type=MESH,
                )
            )
    arrived[own16, :] = outgoing[own16, :]
    notes_in[own8, :] = notes_out[own8, :]
    for c in waits:
        c.wait_recv()
    note = notes_in[0:8, :]
    for s in range(1, N_DP):
        note = note + notes_in[s * 8:(s + 1) * 8, :]
    place_q = jnp.broadcast_to(note[0:1, :], (256, 256)).astype(jnp.int32)
    put = lax.shift_right_logical(sub_q, 5) == (lane_q & 7)
    put = put & ((sub_q & 31) == place_q)
    placed = dot(jnp.where(put, 1.0, 0.0).astype(BF16), arrived[...]).astype(BF16)

    def block(zb, cb, offset=0, size=ROWS_DEV):
        return pl.ds(pl.multiple_of((cb * N_Z + zb) * ROWS_DEV + offset, 16), size)

    def chip(k):
        return lax.rem(z + k + N_Z, N_Z)

    own = block(z, core)
    for h in range(HEADS):
        gathered[own, h * 256:(h + 1) * 256] = placed[h * 32:(h + 1) * 32, :]
    tile = jnp.broadcast_to(note[1:2, 0:128], (8, 128))
    energies[me_l] = tile

    def gather_events(buf, pieces):
        size = ROWS_DEV // pieces
        half = ROWS_DEV // 2
        plan = {}
        for sign in (1, -1):
            for k in range(1, 5):
                if k < 4:
                    parts = [(p * size, size) for p in range(pieces)]
                else:
                    parts = [(0 if sign == 1 else half, half)]
                for off, sz in parts:
                    src_z = chip(-sign * (k - 1))
                    ref = buf.at[block(src_z, core, off, sz)]
                    got = chip(-sign * k)
                    copy = remote(ref, ref, at_z(sign))
                    got_ref = buf.at[block(got, core, off, sz)]
                    arrival = pltpu.make_async_remote_copy(
                        src_ref=got_ref, dst_ref=got_ref, send_sem=send_sems.at[counter[0] - 1],
                        recv_sem=recv_sems.at[counter[0] - 1], device_id=at_z(sign), device_id_type=MESH,
                    )
                    pass_on = remote(got_ref, got_ref, partner)
                    other_ref = buf.at[block(got, other, off, sz)]
                    passed = pltpu.make_async_remote_copy(
                        src_ref=other_ref, dst_ref=other_ref, send_sem=send_sems.at[counter[0] - 1],
                        recv_sem=recv_sems.at[counter[0] - 1], device_id=partner, device_id_type=MESH,
                    )
                    plan[(sign, k, off)] = (copy, arrival, pass_on, passed, sz)
        own_ref = buf.at[own]
        own_pass = remote(own_ref, own_ref, partner)
        own_other = buf.at[block(z, other)]
        own_passed = pltpu.make_async_remote_copy(
            src_ref=own_other, dst_ref=own_other, send_sem=send_sems.at[counter[0] - 1],
            recv_sem=recv_sems.at[counter[0] - 1], device_id=partner, device_id_type=MESH,
        )

        def first():
            for p in range(pieces):
                for sign in (1, -1):
                    start(plan[(sign, 1, p * size)][0])
            start(own_pass)

        def step(k):
            offs = [p * size for p in range(pieces)]
            for n in range(pieces):
                for sign in (1, -1):
                    if k < 4:
                        off = offs[n] if sign == 1 else offs[pieces - 1 - n]
                        off = offs[n]
                    else:
                        if n > 0:
                            continue
                        off = 0 if sign == 1 else half
                    copy, arrival, pass_on, passed, sz = plan[(sign, k, off)]
                    arrival.wait_recv()
                    if k < 3:
                        start(plan[(sign, k + 1, off)][0])
                    elif k == 3:
                        wanted = 0 if sign == 1 else half
                        if pieces == 1 or off == wanted:
                            start(plan[(sign, 4, wanted)][0])
                    start(pass_on)

        def finish(k):
            if k == 0:
                own_passed.wait_recv()
                return
            for key, item in plan.items():
                if key[1] == abs(k) and (abs(k) == 4 or key[0] == (1 if k > 0 else -1)):
                    item[3].wait_recv()

        return first, step, finish

    first, step, finish = gather_events(gathered, 2)
    first()
    e_waits = []
    for o in range(1, N_DP):
        to = lax.rem(me_l + o, N_DP)
        frm = lax.rem(me_l + N_DP - o, N_DP)
        i = counter[0]
        start(remote(energies.at[me_l], energies.at[me_l], {"latent": to}))
        e_waits.append(
            pltpu.make_async_remote_copy(
                src_ref=energies.at[me_l], dst_ref=energies.at[frm], send_sem=send_sems.at[i],
                recv_sem=recv_sems.at[i], device_id={"latent": to}, device_id_type=MESH,
            )
        )

    for c in load_d:
        c.wait()
    diag = iota((128, 128), 0) == iota((128, 128), 1)
    norms = []
    for b in range(LAT // 128):
        total = jnp.zeros((128, 1), F32)
        for j in range(CHUNKS):
            total = total + jnp.sum(jnp.square(dec_v[j, b * 128:(b + 1) * 128, :].astype(F32)), axis=1, keepdims=True)
        norm = jnp.sqrt(total + EPSILON)
        norms.append(norm)
        norm_row[0:1, b * 128:(b + 1) * 128] = SPARSE_SCALE * jnp.sum(
            jnp.where(diag, jnp.broadcast_to(norm, (128, 128)), 0.0), axis=0, keepdims=True
        )
        dec_coef[b * 128:(b + 1) * 128, :] = jnp.broadcast_to(SPARSE_SCALE / norm, (128, 128))

    for c in e_waits:
        c.wait_recv()
    total = energies[0]
    for s in range(1, N_DP):
        total = total + energies[s]
    norm_scale = lax.rsqrt(total[0:1, 0:1] / (ALL_ROWS * WIDTH) + EPSILON)

    load_e.wait()

    def encode(chips):
        spots = [block(zb, cb) for zb in chips for cb in range(2)]
        for n, spot in enumerate(spots):
            scaled = (gathered[spot, :].astype(F32) * norm_scale).astype(BF16)
            inputs[spot, :] = scaled
            batch[n * ROWS_DEV:(n + 1) * ROWS_DEV, :] = scaled

        def tile_step(t, carry):
            at = pl.ds(pl.multiple_of(t * 256, 256), 256)
            pre = 4.0 * (dot(batch[...], enc_v[:, at]) + enc_bias[:, at])
            small = jnp.exp(-jnp.abs(pre))
            active = 0.25 * (jnp.maximum(pre, 0.0) + jnp.log1p(small))
            sig = jnp.where(pre >= 0, 1.0, small) / (1.0 + small)
            act = active.astype(BF16)
            for n, spot in enumerate(spots):
                part = slice(n * ROWS_DEV, (n + 1) * ROWS_DEV)
                coded[spot, at] = act[part, :]
                gate[spot, at] = sig[part, :]
            return carry

        lax.fori_loop(0, LAT // 256, tile_step, 0)

    step(1)
    finish(0)
    finish(1)
    encode((z, chip(-1)))
    step(2)
    finish(-1)
    finish(2)
    encode((chip(1), chip(-2)))
    step(3)
    finish(-2)
    finish(3)
    encode((chip(2), chip(-3)))
    step(4)
    finish(-3)
    finish(4)
    encode((chip(3), chip(4)))

    events = []

    def at_time(t, fn):
        events.append((t, len(events), fn))

    own_half = pl.ds(pl.multiple_of(core * 256, 256), 256)
    other_half = pl.ds(pl.multiple_of(other * 256, 256), 256)
    STEP = 2.3

    def transpose_coded(b):
        def run():
            turned = coded[:, b * 256:(b + 1) * 256].T
            coded_t[b * 256:(b + 1) * 256, :] = turned
            sums = jnp.sum(turned.astype(F32), axis=1, keepdims=True)
            dec_coef[b * 256:(b + 1) * 256, :] = dec_coef[b * 256:(b + 1) * 256, :] * sums
        return run

    def transpose_inputs(j):
        def run():
            for s in range(N_X):
                d = chunk_dp(j, s)
                inputs_t[j, s * 128:(s + 1) * 128, :] = inputs[:, d * 128:(d + 1) * 128].T
        return run

    for b in range(4):
        at_time(5.0 + 2.4 * b, transpose_coded(b))
        at_time(6.2 + 2.4 * b, transpose_inputs(b))

    def latent_stream(j):
        base = 1.0 * j
        swap = remote(part_send.at[j], part_recv.at[j], partner)

        def start_half():
            part_send[j] = dot(coded[other_half, :], dec_v[j]).astype(BF16)
            start(swap)

        def own_part():
            part_own[j] = dot(coded[own_half, :], dec_v[j])

        ring = {}
        for sign, out_buf, in_buf in ((1, rs_send_p, rs_recv_p), (-1, rs_send_m, rs_recv_m)):
            for t in range(4):
                if t == 0:
                    rows = slice(0, 16) if sign == 1 else slice(16, 32)
                else:
                    rows = slice(0, 32)
                ring[(sign, t)] = remote(out_buf.at[j, t, rows], in_buf.at[j, t, rows], at_z(sign))

        def own_block(zb):
            rows = pl.ds(pl.multiple_of(zb * ROWS_DEV, ROWS_DEV), ROWS_DEV)
            return part_own[j, rows, :] + part_recv[j, rows, :].astype(F32)

        def reduce_step(t):
            def run():
                if t == 0:
                    swap.wait_recv()
                for sign, out_buf, in_buf in ((1, rs_send_p, rs_recv_p), (-1, rs_send_m, rs_recv_m)):
                    mine_ = own_block(chip(sign * (4 - t)))
                    near = slice(0, 16) if sign == 1 else slice(16, 32)
                    far = slice(16, 32) if sign == 1 else slice(0, 16)
                    if t == 0:
                        out_buf[j, 0, near, :] = mine_[near, :].astype(BF16)
                    else:
                        ring[(sign, t - 1)].wait_recv()
                        if t == 1:
                            out_buf[j, 1, near, :] = (mine_[near, :] + in_buf[j, 0, near, :].astype(F32)).astype(BF16)
                            out_buf[j, 1, far, :] = mine_[far, :].astype(BF16)
                        else:
                            out_buf[j, t, :, :] = (mine_ + in_buf[j, t - 1, :, :].astype(F32)).astype(BF16)
                    start(ring[(sign, t)])
            return run

        first_, step_, finish_ = gather_events(residual.at[j], 1)

        def own_sum():
            ring[(1, 3)].wait_recv()
            ring[(-1, 3)].wait_recv()
            summed = own_block(z) + rs_recv_p[j, 3, :, :].astype(F32) + rs_recv_m[j, 3, :, :].astype(F32)
            spans = [slice(chunk_dp(j, s) * 128, chunk_dp(j, s) * 128 + 128) for s in range(N_X)]
            bias = jnp.concatenate([dec_bias[:, sp] for sp in spans], axis=1)
            rebuilt = summed + bias
            rebuilt_half = rebuilt.astype(BF16)
            for s, sp in enumerate(spans):
                rebuilt_out[:, sp] = rebuilt_half[:, s * 128:(s + 1) * 128]
            ins = jnp.concatenate([inputs[own, sp] for sp in spans], axis=1).astype(F32)
            residual[j, own, :] = (rebuilt - ins).astype(BF16)
            first_()

        at_time(base, start_half)
        at_time(base + 0.5, own_part)
        for t in range(4):
            at_time(base + 2.5 + t * STEP, reduce_step(t))
        at_time(base + 2.5 + 4 * STEP, own_sum)
        for k in range(1, 5):
            at_time(base + 2.5 + (4 + k) * STEP, lambda k=k: step_(k))

        def all_in():
            finish_(0)
            for k in (1, -1, 2, -2, 3, -3, 4):
                finish_(k)

        return base + 2.5 + 8 * STEP + 1.0, all_in

    def pair_reduce(pick_ref, split, first_in, second_in, hop, me):
        a, b = (0, split), (split, split)
        far = lax.rem(me + 2, N_X)
        up, down = lax.rem(me + 1, N_X), lax.rem(me + 3, N_X)
        full = (0, 2 * split)
        far_up = remote(pick_ref(far, a), first_in.at[0], hop(1))
        far_down = remote(pick_ref(far, b), first_in.at[1], hop(-1))
        near_up = remote(pick_ref(up, full), second_in.at[0], hop(1))
        near_down = remote(pick_ref(down, full), second_in.at[1], hop(-1))

        def go():
            start(far_up)
            start(far_down)

        def combine():
            for copy, place_, part, ref, nxt in (
                (far_up, up, a, first_in.at[0], near_up),
                (far_down, down, b, first_in.at[1], near_down),
            ):
                copy.wait_recv()
                spot = pick_ref(place_, part)
                spot[...] = (spot[...].astype(F32) + ref[...].astype(F32)).astype(BF16)
                start(nxt)

        def total():
            near_up.wait_recv()
            near_down.wait_recv()
            spot = pick_ref(me, full)
            return spot[...].astype(F32) + second_in[0].astype(F32) + second_in[1].astype(F32)

        return go, combine, total

    def grad_stream(term, halves, r1, r2, u, s1, s2, out, rows):
        half = rows // 2
        split = half // 2
        parts = []
        for j in range(CHUNKS):
            both = []
            for o in range(2):
                me = x if o == 0 else y
                hop = at_x if o == 0 else at_y

                def pick_ref(i, part, j=j, o=o):
                    s = i if o == 0 else lax.rem(j - i + N_X, N_X)
                    return term.at[j, s, pl.ds(o * half + part[0], part[1])]

                both.append(pair_reduce(pick_ref, split, r1.at[j, o], r2.at[j, o], hop, me))
            parts.append(both)
        tail = []
        for o in range(2):
            me = y if o == 0 else x
            hop = at_y if o == 0 else at_x

            def pick_ref(i, part, o=o):
                j = lax.rem(i + (x if o == 0 else y), N_X)
                return u.at[o, j, pl.ds(part[0], part[1])]

            tail.append(pair_reduce(pick_ref, split, s1.at[o], s2.at[o], hop, me))

        def fold(j):
            def run():
                for o in range(2):
                    u[o, j] = parts[j][o][2]().astype(BF16)
            return run

        def go(j):
            for o in range(2):
                parts[j][o][0]()

        def combine(j):
            def run():
                for o in range(2):
                    parts[j][o][1]()
            return run

        def tail_go():
            for o in range(2):
                tail[o][0]()

        def tail_combine():
            for o in range(2):
                tail[o][1]()

        def tail_total():
            for o in range(2):
                out[o * half:(o + 1) * half, :] = tail[o][2]()

        return go, combine, fold, tail_go, tail_combine, tail_total

    dec_go, dec_combine, dec_fold, dec_tail_go, dec_tail_combine, dec_tail_total = grad_stream(
        dec_term, None, dec_r1, dec_r2, dec_u, dec_s1, dec_s2, dec_out, LAT
    )
    enc_go, enc_combine, enc_fold, enc_tail_go, enc_tail_combine, enc_tail_total = grad_stream(
        enc_term, None, enc_r1, enc_r2, enc_u, enc_s1, enc_s2, enc_out, 128
    )

    def dec_grad(j):
        def run():
            def tile_step(t, carry):
                at = pl.ds(pl.multiple_of(t * 256, 256), 256)
                term = GRAD_SCALE * dot(coded_t[at, :], residual[j])
                coef = dec_coef[at, :]
                for s in range(N_X):
                    sp = slice(s * 128, (s + 1) * 128)
                    dec_term[j, s, at, :] = (term[:, sp] + coef * dec_v[j, at, sp].astype(F32)).astype(BF16)
                return carry

            lax.fori_loop(0, LAT // 256, tile_step, 0)
            dec_go(j)
        return run

    def act_grad(j):
        def run():
            def tile_step(t, carry):
                at = pl.ds(pl.multiple_of(t * 256, 256), 256)
                part = dot_nt(residual[j], dec_v[j, at, :])
                if j == 0:
                    grad_act[:, at] = part
                elif j < CHUNKS - 1:
                    grad_act[:, at] = grad_act[:, at] + part
                else:
                    whole = GRAD_SCALE * (grad_act[:, at] + part) + norm_row[0:1, at]
                    grad_pre[:, at] = (whole * gate[:, at]).astype(BF16)
                return carry

            lax.fori_loop(0, LAT // 256, tile_step, 0)
        return run

    def enc_grad(j):
        def run():
            def tile_step(t, carry):
                at = pl.ds(pl.multiple_of(t * 256, 256), 256)
                term = dot(inputs_t[j], grad_pre[:, at]).astype(BF16)
                for s in range(N_X):
                    enc_term[j, s, :, at] = term[s * 128:(s + 1) * 128, :]
                return carry

            lax.fori_loop(0, LAT // 256, tile_step, 0)
            enc_go(j)
        return run

    WIRE = 4.2
    ready = 0.0
    for j in range(CHUNKS):
        t, all_in = latent_stream(j)
        ready = max(t, ready + 2.0)
        at_time(ready, all_in)
        at_time(ready + 0.1, dec_grad(j))
        at_time(ready + 0.2, act_grad(j))
        at_time(ready + 4.5, dec_combine(j))
        at_time(ready + 9.0, dec_fold(j))
    dec_end = ready + 9.0
    enc_start = ready + 2.0
    for j in range(CHUNKS):
        t = enc_start + 1.0 * j
        at_time(t, enc_grad(j))
        at_time(t + 5.0 + (WIRE - 1.0) * j, enc_combine(j))
        at_time(t + 9.5 + (WIRE - 1.0) * j, enc_fold(j))
    enc_end = enc_start + 9.5 + WIRE * 3
    at_time(dec_end + 0.1, dec_tail_go)
    at_time(dec_end + 5.0, dec_tail_combine)
    at_time(dec_end + 12.0, dec_tail_total)
    at_time(enc_end + 0.1, enc_tail_go)
    at_time(enc_end + 3.5, enc_tail_combine)
    at_time(enc_end + 8.0, enc_tail_total)

    for _, _, fn in sorted(events, key=lambda e: (e[0], e[1])):
        fn()
    for copy in sent:
        copy.wait_send()


def shards(
    queries, cache_keys, cache_values, positions, shuffle, enc_weight, enc_bias, dec_weight, dec_bias
):
    any_ = pl.BlockSpec(memory_space=pl.ANY)
    vmem = pl.BlockSpec(memory_space=pltpu.VMEM)
    quarter = ROWS_DEV // 2
    scratch = [
        ((ROWS_DEV, WIDTH), BF16),
        ((CACHE, KV_HEADS * HEAD_DIM), BF16),
        ((CACHE, KV_HEADS * HEAD_DIM), BF16),
        ((WIDTH, LAT), BF16),
        ((CHUNKS, LAT, COLS), BF16),
        ((256, 256), BF16),
        ((256, 256), BF16),
        ((256, 256), BF16),
        ((128, 256), F32),
        ((128, 256), F32),
        ((16, 8, 128), F32),
        ((GROUP, WIDTH), BF16),
        ((GROUP, WIDTH), BF16),
        ((128, WIDTH), BF16),
        ((CHUNKS, COLS, GROUP), BF16),
        ((GROUP, LAT), BF16),
        ((LAT, GROUP), BF16),
        ((GROUP, LAT), F32),
        ((8, LAT), F32),
        ((LAT, 128), F32),
        ((CHUNKS, 256, COLS), BF16),
        ((CHUNKS, 256, COLS), BF16),
        ((CHUNKS, 256, COLS), F32),
        ((CHUNKS, 4, ROWS_DEV, COLS), BF16),
        ((CHUNKS, 4, ROWS_DEV, COLS), BF16),
        ((CHUNKS, 4, ROWS_DEV, COLS), BF16),
        ((CHUNKS, 4, ROWS_DEV, COLS), BF16),
        ((CHUNKS, GROUP, COLS), BF16),
        ((GROUP, LAT), F32),
        ((GROUP, LAT), BF16),
        ((CHUNKS, 4, LAT, 128), BF16),
        ((CHUNKS, 4, 128, LAT), BF16),
        ((CHUNKS, 2, 2, 256, 128), BF16),
        ((CHUNKS, 2, 2, 512, 128), BF16),
        ((CHUNKS, 2, 2, 32, LAT), BF16),
        ((CHUNKS, 2, 2, 64, LAT), BF16),
        ((2, CHUNKS, 512, 128), BF16),
        ((2, CHUNKS, 64, LAT), BF16),
        ((2, 2, 256, 128), BF16),
        ((2, 2, 512, 128), BF16),
        ((2, 2, 32, LAT), BF16),
        ((2, 2, 64, LAT), BF16),
    ]
    return pl.pallas_call(
        kernel,
        out_shape=(
            jax.ShapeDtypeStruct((ROWS_DEV, WIDTH), BF16),
            jax.ShapeDtypeStruct((128, LAT), F32),
            jax.ShapeDtypeStruct((LAT, 128), F32),
        ),
        in_specs=[any_, any_, any_, vmem, vmem, any_, vmem, any_, vmem],
        out_specs=(vmem, vmem, vmem),
        scratch_shapes=[pltpu.VMEM(shape, dtype) for shape, dtype in scratch]
        + [
            pltpu.SemaphoreType.DMA((N_SEMS,)),
            pltpu.SemaphoreType.DMA((N_SEMS,)),
            pltpu.SemaphoreType.DMA((20,)),
        ],
        compiler_params=pltpu.CompilerParams(
            collective_id=0, has_side_effects=True, vmem_limit_bytes=67043328
        ),
    )(
        queries, cache_keys, cache_values, positions.reshape(1, -1), shuffle.reshape(1, -1),
        enc_weight, enc_bias.reshape(1, -1), dec_weight, dec_bias.reshape(1, -1),
    )


def solution(mesh):
    in_specs = (
        P(("dp", "latent"), None),
        P(("dp", "latent"), None, None),
        P(("dp", "latent"), None, None),
        P(("dp", "latent")),
        P(("dp", "latent")),
        P(None, "latent"),
        P("latent"),
        P("latent", None),
        P(),
    )
    out_specs = (P(("dp", "latent"), None), P("dp", "latent"), P("latent", "dp"))
    return jax.shard_map(shards, mesh=mesh, in_specs=in_specs, out_specs=out_specs, check_vma=False)
```

```python
import jax
import jax.numpy as jnp
from jax import lax
from jax.experimental import pallas as pl
from jax.experimental.pallas import tpu as pltpu
from jax.sharding import PartitionSpec as P

F32 = jnp.float32
BF16 = jnp.bfloat16
MESH = pl.DeviceIdType.MESH

HEAD_DIM = 256
KV_HEADS = 4
HEADS = 8
CACHE = 512
ROWS_DEV = 32
GROUP = 512
WIDTH = 2048
LAT = 1024
ALL_ROWS = 8192
N_X = 4
N_Z = 8
N_DP = 16
CHUNKS = 4
COLS = WIDTH // CHUNKS
EPSILON = 1e-06
GRAD_SCALE = 2.0 / ALL_ROWS
SPARSE_SCALE = 1.0 / ALL_ROWS

N_SEMS = 300


def dot(a, b):
    return jnp.dot(a, b, preferred_element_type=F32)


def dot_nt(a, b):
    return lax.dot_general(a, b, (((1,), (1,)), ((), ())), preferred_element_type=F32)


def iota(shape, axis):
    return lax.broadcasted_iota(jnp.int32, shape, axis)


def chunk_dp(j, s):
    return s * N_X + (j - s) % N_X


def kernel(
    queries, keys, values, positions, shuffle, enc_w, enc_bias, dec_w, dec_bias,
    rebuilt_out, enc_out, dec_out,
    q_v, k_v, v_v, enc_v, dec_v, heads, outgoing, arrived, notes_out, notes_in,
    energies, gathered, inputs, batch, inputs_t, coded, coded_t, gate, norm_row, dec_coef,
    part_send, part_recv, part_own, rs_send_p, rs_recv_p, rs_send_m, rs_recv_m,
    residual, grad_act, grad_pre, dec_term, enc_term,
    dec_r1, dec_r2, enc_r1, enc_r2, dec_u, enc_u, dec_s1, dec_s2, enc_s1, enc_s2,
    send_sems, recv_sems, local_sems,
):
    me_dp = lax.axis_index("dp")
    me_l = lax.axis_index("latent")
    x, y = me_dp // N_X, me_dp % N_X
    z, core = me_l // 2, me_l % 2
    other = 1 - core

    def at_z(k):
        return {"latent": lax.rem(z + k + N_Z, N_Z) * 2 + core}

    partner = {"latent": z * 2 + other}

    def at_x(k):
        return {"dp": lax.rem(x + k + N_X, N_X) * N_X + y}

    def at_y(k):
        return {"dp": x * N_X + lax.rem(y + k + N_X, N_X)}

    counter = [0]
    sent = []

    def remote(src, dst, device):
        i = counter[0]
        counter[0] += 1
        return pltpu.make_async_remote_copy(
            src_ref=src, dst_ref=dst, send_sem=send_sems.at[i], recv_sem=recv_sems.at[i],
            device_id=device, device_id_type=MESH,
        )

    def start(copy):
        copy.start()
        sent.append(copy)
        return copy

    def load(src, dst, i):
        c = pltpu.make_async_copy(src, dst, local_sems.at[i])
        c.start()
        return c

    load_q = load(queries, q_v, 0)
    load_k = load(keys.at[0], k_v, 1)
    load_v = load(values.at[0], v_v, 2)
    load_e = load(enc_w, enc_v, 3)
    load_d = []
    for j in range(CHUNKS):
        for s in range(N_X):
            d = chunk_dp(j, s)
            load_d.append(
                load(dec_w.at[:, d * 128:(d + 1) * 128], dec_v.at[j, :, s * 128:(s + 1) * 128], 4 + j * N_X + s)
            )

    barrier = pltpu.get_barrier_semaphore()
    for o in range(1, N_DP):
        pl.semaphore_signal(barrier, inc=1, device_id={"dp": lax.rem(me_dp + o, N_DP)}, device_id_type=MESH)
        pl.semaphore_signal(barrier, inc=1, device_id={"latent": lax.rem(me_l + o, N_DP)}, device_id_type=MESH)

    shuffle_row = shuffle[...]
    sub = iota((ROWS_DEV, ROWS_DEV), 0)
    lane = iota((ROWS_DEV, ROWS_DEV), 1)
    eye = sub == lane
    wide = jnp.broadcast_to(shuffle_row, (ROWS_DEV, ROWS_DEV))
    shuffle_col = jnp.sum(jnp.where(eye, wide.astype(F32), 0.0), axis=1, keepdims=True).astype(jnp.int32)
    target_row = lax.shift_right_logical(wide, 9)
    target_col = lax.shift_right_logical(shuffle_col, 9)
    before = jnp.where((target_row == target_col) & (lane < sub), 1.0, 0.0)
    slot_col = 2.0 * target_col.astype(F32) + jnp.sum(before, axis=1, keepdims=True)
    lane_w = iota((ROWS_DEV, 256), 1)
    sub_w = iota((ROWS_DEV, 256), 0)
    slot_wide = jnp.sum(
        jnp.where((lane_w & 31) == sub_w, jnp.broadcast_to(slot_col, (ROWS_DEV, 256)), 0.0), axis=0, keepdims=True
    ).astype(jnp.int32)
    slot_row = jnp.sum(jnp.where(eye, jnp.broadcast_to(slot_col, (ROWS_DEV, ROWS_DEV)), 0.0), axis=0, keepdims=True)
    slot_row = slot_row.astype(jnp.int32)
    place_row = (shuffle_row & 31).astype(F32)
    sub_q = iota((256, 256), 0)
    lane_q = iota((256, 256), 1)
    pick = (sub_q & 7) == lax.shift_right_logical(lane_q, 5)
    pick = pick & (lax.shift_right_logical(sub_q, 3) == slot_wide)
    pick = jnp.where(pick, 1.0, 0.0).astype(BF16)

    pos_wide = jnp.broadcast_to(positions[...], (ROWS_DEV, ROWS_DEV)).astype(F32)
    pos_col = jnp.sum(jnp.where(eye, pos_wide, 0.0), axis=1, keepdims=True).astype(jnp.int32)
    pos_col = jnp.concatenate([pos_col, pos_col], axis=0)
    visible = iota((2 * ROWS_DEV, CACHE), 1) <= pos_col
    load_q.wait()
    load_k.wait()
    load_v.wait()
    energy = jnp.zeros((1, 1), F32)
    for g in range(KV_HEADS):
        cols = slice(g * HEAD_DIM, (g + 1) * HEAD_DIM)
        pair = jnp.concatenate(
            [q_v[:, (2 * g + i) * HEAD_DIM:(2 * g + i + 1) * HEAD_DIM] for i in range(2)], axis=0
        )
        scores = dot_nt(pair, k_v[:, cols]) * HEAD_DIM ** (-0.5)
        scores = jnp.where(visible, scores, -jnp.inf)
        weights = jnp.exp(scores - jnp.max(scores, axis=1, keepdims=True))
        probs = (weights / jnp.sum(weights, axis=1, keepdims=True)).astype(BF16)
        mixed = dot(probs, v_v[:, cols]).astype(BF16)
        heads[g * 64:(g + 1) * 64, :] = mixed
        square = jnp.square(mixed.astype(F32))
        energy = energy + jnp.sum(jnp.sum(square, axis=1, keepdims=True), axis=0, keepdims=True)
    outgoing[...] = dot(pick, heads[...]).astype(BF16)

    note_sub = iota((128, 256), 0)
    note_lane = iota((128, 256), 1)
    peer_sub = lax.shift_right_logical(iota((128, ROWS_DEV), 0), 3)
    slot_n = jnp.broadcast_to(slot_row, (128, ROWS_DEV))
    place_n = jnp.broadcast_to(place_row, (128, ROWS_DEV))
    place = [
        jnp.sum(jnp.where(slot_n == 2 * peer_sub + k, place_n, 0.0), axis=1, keepdims=True) for k in range(2)
    ]
    mine = lax.shift_right_logical(note_lane, 4) == me_dp
    place_note = jnp.where((lax.shift_right_logical(note_lane, 3) & 1) == 0, place[0], place[1])
    place_note = jnp.where(mine, place_note, 0.0)
    notes_out[...] = jnp.where((note_sub & 7) == 0, place_note, jnp.broadcast_to(energy, (128, 256)))

    pl.semaphore_wait(barrier, 2 * (N_DP - 1))
    own16 = pl.ds(pl.multiple_of(me_dp * 16, 16), 16)
    own8 = pl.ds(pl.multiple_of(me_dp * 8, 8), 8)
    waits = []
    for o in range(1, N_DP):
        to = lax.rem(me_dp + o, N_DP)
        frm = lax.rem(me_dp + N_DP - o, N_DP)
        to16 = pl.ds(pl.multiple_of(to * 16, 16), 16)
        to8 = pl.ds(pl.multiple_of(to * 8, 8), 8)
        frm16 = pl.ds(pl.multiple_of(frm * 16, 16), 16)
        frm8 = pl.ds(pl.multiple_of(frm * 8, 8), 8)
        for src, dst, to_at, own_at, frm_at in (
            (outgoing, arrived, to16, own16, frm16),
            (notes_out, notes_in, to8, own8, frm8),
        ):
            i = counter[0]
            c = start(remote(src.at[to_at], dst.at[own_at], {"dp": to}))
            waits.append(
                pltpu.make_async_remote_copy(
                    src_ref=src.at[to_at], dst_ref=dst.at[frm_at], send_sem=send_sems.at[i],
                    recv_sem=recv_sems.at[i], device_id={"dp": to}, device_id_type=MESH,
                )
            )
    arrived[own16, :] = outgoing[own16, :]
    notes_in[own8, :] = notes_out[own8, :]
    for c in load_d:
        c.wait()
    diag = iota((128, 128), 0) == iota((128, 128), 1)
    norms = []
    for b in range(LAT // 128):
        total = jnp.zeros((128, 1), F32)
        for j in range(CHUNKS):
            total = total + jnp.sum(jnp.square(dec_v[j, b * 128:(b + 1) * 128, :].astype(F32)), axis=1, keepdims=True)
        norm = jnp.sqrt(total + EPSILON)
        norms.append(norm)
        norm_row[0:1, b * 128:(b + 1) * 128] = SPARSE_SCALE * jnp.sum(
            jnp.where(diag, jnp.broadcast_to(norm, (128, 128)), 0.0), axis=0, keepdims=True
        )
        dec_coef[b * 128:(b + 1) * 128, :] = jnp.broadcast_to(SPARSE_SCALE / norm, (128, 128))

    for c in waits:
        c.wait_recv()
    note = notes_in[0:8, :]
    for s in range(1, N_DP):
        note = note + notes_in[s * 8:(s + 1) * 8, :]
    place_q = jnp.broadcast_to(note[0:1, :], (256, 256)).astype(jnp.int32)
    put = lax.shift_right_logical(sub_q, 5) == (lane_q & 7)
    put = put & ((sub_q & 31) == place_q)
    placed = dot(jnp.where(put, 1.0, 0.0).astype(BF16), arrived[...]).astype(BF16)

    def block(zb, cb, offset=0, size=ROWS_DEV):
        return pl.ds(pl.multiple_of((cb * N_Z + zb) * ROWS_DEV + offset, 16), size)

    def chip(k):
        return lax.rem(z + k + N_Z, N_Z)

    own = block(z, core)
    half = ROWS_DEV // 2

    def hop(buf, zb, offset, size, device, arrives):
        ref = buf.at[block(zb, core, offset, size)]
        copy = remote(ref, ref, device)
        got_ref = buf.at[block(arrives, core, offset, size)]
        arrival = same_semaphores(got_ref, device)
        pass_on = remote(got_ref, got_ref, partner)
        passed = same_semaphores(buf.at[block(arrives, other, offset, size)], partner)
        return copy, arrival, pass_on, passed

    def same_semaphores(ref, device):
        i = counter[0] - 1
        return pltpu.make_async_remote_copy(
            src_ref=ref, dst_ref=ref, send_sem=send_sems.at[i], recv_sem=recv_sems.at[i],
            device_id=device, device_id_type=MESH,
        )

    def own_hop(buf):
        pass_on = remote(buf.at[own], buf.at[own], partner)
        return pass_on, same_semaphores(buf.at[block(z, other)], partner)

    def ring_gather(buf):
        plan = {}
        for k in range(1, 5):
            for sign in (1, -1):
                off, size = (0, ROWS_DEV) if k < 4 else (0 if sign == 1 else half, half)
                plan[(sign, k)] = hop(buf, chip(-sign * (k - 1)), off, size, at_z(sign), chip(-sign * k))
        own_pass, own_passed = own_hop(buf)

        def first():
            start(plan[(1, 1)][0])
            start(plan[(-1, 1)][0])
            start(own_pass)

        def step(k):
            for sign in (1, -1):
                plan[(sign, k)][1].wait_recv()
                if k < 4:
                    start(plan[(sign, k + 1)][0])
                start(plan[(sign, k)][2])

        def finish(k):
            if k == 0:
                own_passed.wait_recv()
            elif abs(k) == 4:
                plan[(1, 4)][3].wait_recv()
                plan[(-1, 4)][3].wait_recv()
            else:
                plan[(1 if k < 0 else -1, abs(k))][3].wait_recv()

        return first, step, finish

    def quick_gather(buf):
        near, far, third, fourth = {}, {}, {}, {}
        for sign in (1, -1):
            far[sign] = hop(buf, z, 0, ROWS_DEV, at_z(2 * sign), chip(-2 * sign))
            near[sign] = hop(buf, z, 0, ROWS_DEV, at_z(sign), chip(-sign))
            third[sign] = hop(buf, chip(-2 * sign), 0, ROWS_DEV, at_z(sign), chip(-3 * sign))
            fourth[sign] = hop(buf, chip(-2 * sign), 0 if sign == 1 else half, half, at_z(2 * sign), chip(4))
        own_pass, own_passed = own_hop(buf)

        def first():
            for group in (far, near):
                for sign in (1, -1):
                    start(group[sign][0])
            start(own_pass)

        def middle():
            for sign in (1, -1):
                far[sign][1].wait_recv()
                start(fourth[sign][0])
                start(third[sign][0])
                start(far[sign][2])
            for sign in (1, -1):
                near[sign][1].wait_recv()
                start(near[sign][2])

        def last():
            for group in (third, fourth):
                for sign in (1, -1):
                    group[sign][1].wait_recv()
                    start(group[sign][2])

        def finish():
            own_passed.wait_recv()
            for group in (far, near, third, fourth):
                for sign in (1, -1):
                    group[sign][3].wait_recv()

        return first, middle, last, finish

    for h in range(HEADS):
        gathered[h // 2, own, (h % 2) * 256:(h % 2 + 1) * 256] = placed[h * 32:(h + 1) * 32, :]
    energies[me_l] = jnp.broadcast_to(note[1:2, 0:128], (8, 128))
    e_waits = []
    for o in range(1, N_DP):
        to = lax.rem(me_l + o, N_DP)
        frm = lax.rem(me_l + N_DP - o, N_DP)
        start(remote(energies.at[me_l], energies.at[me_l], {"latent": to}))
        e_waits.append(same_semaphores(energies.at[frm], {"latent": to}))
    rings = [ring_gather(gathered.at[c]) for c in range(CHUNKS)]

    def step(k):
        for ring in rings:
            ring[1](k)

    def finish(*ks):
        for ring in rings:
            for k in ks:
                ring[2](k)

    for ring in rings:
        ring[0]()
    step(1)
    for c in e_waits:
        c.wait_recv()
    total = energies[0]
    for s in range(1, N_DP):
        total = total + energies[s]
    norm_scale = lax.rsqrt(total[0:1, 0:1] / (ALL_ROWS * WIDTH) + EPSILON)

    load_e.wait()

    def encode(chips):
        spots = [block(zb, cb) for zb in chips for cb in range(2)]
        for n, spot in enumerate(spots):
            for c in range(CHUNKS):
                scaled = (gathered[c, spot, :].astype(F32) * norm_scale).astype(BF16)
                inputs[spot, c * COLS:(c + 1) * COLS] = scaled
                batch[n * ROWS_DEV:(n + 1) * ROWS_DEV, c * COLS:(c + 1) * COLS] = scaled

        def tile_step(t, carry):
            at = pl.ds(pl.multiple_of(t * 256, 256), 256)
            pre = 4.0 * (dot(batch[...], enc_v[:, at]) + enc_bias[:, at])
            small = jnp.exp(-jnp.abs(pre))
            active = 0.25 * (jnp.maximum(pre, 0.0) + jnp.log1p(small))
            sig = jnp.where(pre >= 0, 1.0, small) / (1.0 + small)
            act = active.astype(BF16)
            for n, spot in enumerate(spots):
                part = slice(n * ROWS_DEV, (n + 1) * ROWS_DEV)
                coded[spot, at] = act[part, :]
                gate[spot, at] = sig[part, :]
            return carry

        lax.fori_loop(0, LAT // 256, tile_step, 0)

    step(2)
    finish(0, -1)
    encode((z, chip(-1)))
    step(3)
    finish(1, -2)
    encode((chip(1), chip(-2)))
    finish(2, -3)
    encode((chip(2), chip(-3)))
    step(4)
    finish(3, 4)
    encode((chip(3), chip(4)))

    events = []

    def at_time(t, fn):
        events.append((t, len(events), fn))

    own_half = pl.ds(pl.multiple_of(core * 256, 256), 256)
    other_half = pl.ds(pl.multiple_of(other * 256, 256), 256)

    def transpose_coded(b):
        def run():
            turned = coded[:, b * 256:(b + 1) * 256].T
            coded_t[b * 256:(b + 1) * 256, :] = turned
            sums = jnp.sum(turned.astype(F32), axis=1, keepdims=True)
            dec_coef[b * 256:(b + 1) * 256, :] = dec_coef[b * 256:(b + 1) * 256, :] * sums
        return run

    def transpose_inputs(j):
        def run():
            for s in range(N_X):
                d = chunk_dp(j, s)
                inputs_t[j, s * 128:(s + 1) * 128, :] = inputs[:, d * 128:(d + 1) * 128].T
        return run

    for b in range(4):
        at_time((2.5, 2.6, 4.5, 4.6)[b], transpose_coded(b))
        at_time((6.5, 9.0, 11.0, 13.2)[b], transpose_inputs(b))

    def latent_stream(j):
        begin = (0.0, 1.0, 3.0, 7.0)[j]
        base = (2.2, 4.2, 8.4, 12.8)[j]
        swap = remote(part_send.at[j], part_recv.at[j], partner)

        def start_half():
            part_send[j] = dot(coded[other_half, :], dec_v[j]).astype(BF16)
            start(swap)

        def own_part():
            part_own[j] = dot(coded[own_half, :], dec_v[j])

        sides = ((1, rs_send_p, rs_recv_p), (-1, rs_send_m, rs_recv_m))
        hops = {}
        for sign, out_buf, in_buf in sides:
            near = slice(0, 16) if sign == 1 else slice(16, 32)
            for slot, dist in ((0, 2), (1, 1), (2, 2), (3, 1)):
                rows = near if slot == 0 else slice(0, 32)
                hops[(sign, slot)] = remote(out_buf.at[j, slot, rows], in_buf.at[j, slot, rows], at_z(dist * sign))

        def own_block(zb):
            rows = pl.ds(pl.multiple_of(zb * ROWS_DEV, ROWS_DEV), ROWS_DEV)
            return part_own[j, rows, :] + part_recv[j, rows, :].astype(F32)

        def reduce_first():
            swap.wait_recv()
            for slot, dist in ((0, 4), (1, 3), (3, 1)):
                for sign, out_buf, in_buf in sides:
                    mine_ = own_block(chip(sign * dist))
                    near = slice(0, 16) if sign == 1 else slice(16, 32)
                    rows = near if slot == 0 else slice(0, 32)
                    out_buf[j, slot, rows, :] = mine_[rows, :].astype(BF16)
                    start(hops[(sign, slot)])

        def reduce_second():
            for sign, out_buf, in_buf in sides:
                near = slice(0, 16) if sign == 1 else slice(16, 32)
                far = slice(16, 32) if sign == 1 else slice(0, 16)
                hops[(sign, 1)].wait_recv()
                hops[(sign, 0)].wait_recv()
                mine_ = own_block(chip(sign * 2)) + in_buf[j, 1, :, :].astype(F32)
                out_buf[j, 2, near, :] = (mine_[near, :] + in_buf[j, 0, near, :].astype(F32)).astype(BF16)
                out_buf[j, 2, far, :] = mine_[far, :].astype(BF16)
                start(hops[(sign, 2)])

        first_, middle_, last_, finish_ = quick_gather(residual.at[j])

        def own_sum():
            summed = own_block(z)
            for slot in (3, 2):
                for sign, out_buf, in_buf in sides:
                    hops[(sign, slot)].wait_recv()
                    summed = summed + in_buf[j, slot, :, :].astype(F32)
            spans = [slice(chunk_dp(j, s) * 128, chunk_dp(j, s) * 128 + 128) for s in range(N_X)]
            bias = jnp.concatenate([dec_bias[:, sp] for sp in spans], axis=1)
            rebuilt = summed + bias
            rebuilt_half = rebuilt.astype(BF16)
            for s, sp in enumerate(spans):
                rebuilt_out[:, sp] = rebuilt_half[:, s * 128:(s + 1) * 128]
            ins = jnp.concatenate([inputs[own, sp] for sp in spans], axis=1).astype(F32)
            residual[j, own, :] = (rebuilt - ins).astype(BF16)
            first_()

        at_time(begin, start_half)
        at_time(begin + 0.5, own_part)
        at_time(base, reduce_first)
        at_time(base + 4.0, reduce_second)
        at_time(base + 8.2, own_sum)
        at_time(base + 12.6, middle_)
        at_time(base + 16.8, last_)
        return base + 18.2, finish_

    def pair_reduce(pick_ref, split, first_in, second_in, hop, me):
        a, b = (0, split), (split, split)
        far = lax.rem(me + 2, N_X)
        up, down = lax.rem(me + 1, N_X), lax.rem(me + 3, N_X)
        full = (0, 2 * split)
        far_up = remote(pick_ref(far, a), first_in.at[0], hop(1))
        far_down = remote(pick_ref(far, b), first_in.at[1], hop(-1))
        near_up = remote(pick_ref(up, full), second_in.at[0], hop(1))
        near_down = remote(pick_ref(down, full), second_in.at[1], hop(-1))

        def go():
            start(far_up)
            start(far_down)

        def combine():
            for copy, place_, part, ref, nxt in (
                (far_up, up, a, first_in.at[0], near_up),
                (far_down, down, b, first_in.at[1], near_down),
            ):
                copy.wait_recv()
                spot = pick_ref(place_, part)
                spot[...] = (spot[...].astype(F32) + ref[...].astype(F32)).astype(BF16)
                start(nxt)

        def total():
            near_up.wait_recv()
            near_down.wait_recv()
            spot = pick_ref(me, full)
            return spot[...].astype(F32) + second_in[0].astype(F32) + second_in[1].astype(F32)

        return go, combine, total

    def grad_stream(term, halves, r1, r2, u, s1, s2, out, rows):
        half = rows // 2
        split = half // 2
        parts = []
        for j in range(CHUNKS):
            both = []
            for o in range(2):
                me = x if o == 0 else y
                hop = at_x if o == 0 else at_y

                def pick_ref(i, part, j=j, o=o):
                    s = i if o == 0 else lax.rem(j - i + N_X, N_X)
                    return term.at[j, s, pl.ds(o * half + part[0], part[1])]

                both.append(pair_reduce(pick_ref, split, r1.at[j, o], r2.at[j, o], hop, me))
            parts.append(both)
        tail = []
        for o in range(2):
            me = y if o == 0 else x
            hop = at_y if o == 0 else at_x

            def pick_ref(i, part, o=o):
                j = lax.rem(i + (x if o == 0 else y), N_X)
                return u.at[o, j, pl.ds(part[0], part[1])]

            tail.append(pair_reduce(pick_ref, split, s1.at[o], s2.at[o], hop, me))

        def fold(j):
            def run():
                for o in range(2):
                    u[o, j] = parts[j][o][2]().astype(BF16)
            return run

        def go(j):
            for o in range(2):
                parts[j][o][0]()

        def combine(j):
            def run():
                for o in range(2):
                    parts[j][o][1]()
            return run

        def tail_go():
            for o in range(2):
                tail[o][0]()

        def tail_combine():
            for o in range(2):
                tail[o][1]()

        def tail_total():
            for o in range(2):
                out[o * half:(o + 1) * half, :] = tail[o][2]()

        return go, combine, fold, tail_go, tail_combine, tail_total

    dec_go, dec_combine, dec_fold, dec_tail_go, dec_tail_combine, dec_tail_total = grad_stream(
        dec_term, None, dec_r1, dec_r2, dec_u, dec_s1, dec_s2, dec_out, LAT
    )
    enc_go, enc_combine, enc_fold, enc_tail_go, enc_tail_combine, enc_tail_total = grad_stream(
        enc_term, None, enc_r1, enc_r2, enc_u, enc_s1, enc_s2, enc_out, 128
    )

    def dec_grad(j):
        def run():
            def tile_step(t, carry):
                at = pl.ds(pl.multiple_of(t * 256, 256), 256)
                term = GRAD_SCALE * dot(coded_t[at, :], residual[j])
                coef = dec_coef[at, :]
                for s in range(N_X):
                    sp = slice(s * 128, (s + 1) * 128)
                    dec_term[j, s, at, :] = (term[:, sp] + coef * dec_v[j, at, sp].astype(F32)).astype(BF16)
                return carry

            lax.fori_loop(0, LAT // 256, tile_step, 0)
            dec_go(j)
        return run

    def act_grad(j):
        def run():
            def tile_step(t, carry):
                at = pl.ds(pl.multiple_of(t * 256, 256), 256)
                part = dot_nt(residual[j], dec_v[j, at, :])
                if j == 0:
                    grad_act[:, at] = part
                elif j < CHUNKS - 1:
                    grad_act[:, at] = grad_act[:, at] + part
                else:
                    whole = GRAD_SCALE * (grad_act[:, at] + part) + norm_row[0:1, at]
                    grad_pre[:, at] = (whole * gate[:, at]).astype(BF16)
                return carry

            lax.fori_loop(0, LAT // 256, tile_step, 0)
        return run

    def enc_grad(j):
        def run():
            def tile_step(t, carry):
                at = pl.ds(pl.multiple_of(t * 256, 256), 256)
                term = dot(inputs_t[j], grad_pre[:, at]).astype(BF16)
                for s in range(N_X):
                    enc_term[j, s, :, at] = term[s * 128:(s + 1) * 128, :]
                return carry

            lax.fori_loop(0, LAT // 256, tile_step, 0)
            enc_go(j)
        return run

    WIRE = 4.2
    ready = 0.0
    for j in range(CHUNKS):
        t, all_in = latent_stream(j)
        ready = max(t, ready + 2.0)
        at_time(ready, all_in)
        at_time(ready + 0.1, dec_grad(j))
        at_time(ready + 0.2, act_grad(j))
        at_time(ready + 4.5, dec_combine(j))
        at_time(ready + 9.0, dec_fold(j))
    dec_end = ready + 9.0
    enc_start = ready + 2.0
    for j in range(CHUNKS):
        t = enc_start + 1.0 * j
        at_time(t, enc_grad(j))
        at_time(t + 5.0 + (WIRE - 1.0) * j, enc_combine(j))
        at_time(t + 9.5 + (WIRE - 1.0) * j, enc_fold(j))
    enc_end = enc_start + 9.5 + WIRE * 3
    at_time(dec_end + 0.1, dec_tail_go)
    at_time(dec_end + 5.0, dec_tail_combine)
    at_time(dec_end + 12.0, dec_tail_total)
    at_time(enc_end + 0.1, enc_tail_go)
    at_time(enc_end + 3.5, enc_tail_combine)
    at_time(enc_end + 8.0, enc_tail_total)

    for _, _, fn in sorted(events, key=lambda e: (e[0], e[1])):
        fn()
    for copy in sent:
        copy.wait_send()


def finish_kernel(*refs):
    ins, outs, bufs, sems = refs[0:3], refs[3:6], refs[6:9], refs[9]
    loads = [pltpu.make_async_copy(a, b, sems.at[0, i]) for i, (a, b) in enumerate(zip(ins, bufs))]
    stores = [pltpu.make_async_copy(a, b, sems.at[1, i]) for i, (a, b) in enumerate(zip(bufs, outs))]
    for c in loads:
        c.start()
    for a, b in zip(loads, stores):
        a.wait()
        b.start()
    for c in stores:
        c.wait()


def shards(
    queries, cache_keys, cache_values, positions, shuffle, enc_weight, enc_bias, dec_weight, dec_bias
):
    any_ = pl.BlockSpec(memory_space=pl.ANY)
    vmem = pl.BlockSpec(memory_space=pltpu.VMEM)
    scratch = [
        ((ROWS_DEV, WIDTH), BF16),
        ((CACHE, KV_HEADS * HEAD_DIM), BF16),
        ((CACHE, KV_HEADS * HEAD_DIM), BF16),
        ((WIDTH, LAT), BF16),
        ((CHUNKS, LAT, COLS), BF16),
        ((256, 256), BF16),
        ((256, 256), BF16),
        ((256, 256), BF16),
        ((128, 256), F32),
        ((128, 256), F32),
        ((16, 8, 128), F32),
        ((CHUNKS, GROUP, COLS), BF16),
        ((GROUP, WIDTH), BF16),
        ((128, WIDTH), BF16),
        ((CHUNKS, COLS, GROUP), BF16),
        ((GROUP, LAT), BF16),
        ((LAT, GROUP), BF16),
        ((GROUP, LAT), F32),
        ((8, LAT), F32),
        ((LAT, 128), F32),
        ((CHUNKS, 256, COLS), BF16),
        ((CHUNKS, 256, COLS), BF16),
        ((CHUNKS, 256, COLS), F32),
        ((CHUNKS, 4, ROWS_DEV, COLS), BF16),
        ((CHUNKS, 4, ROWS_DEV, COLS), BF16),
        ((CHUNKS, 4, ROWS_DEV, COLS), BF16),
        ((CHUNKS, 4, ROWS_DEV, COLS), BF16),
        ((CHUNKS, GROUP, COLS), BF16),
        ((GROUP, LAT), F32),
        ((GROUP, LAT), BF16),
        ((CHUNKS, 4, LAT, 128), BF16),
        ((CHUNKS, 4, 128, LAT), BF16),
        ((CHUNKS, 2, 2, 256, 128), BF16),
        ((CHUNKS, 2, 2, 512, 128), BF16),
        ((CHUNKS, 2, 2, 32, LAT), BF16),
        ((CHUNKS, 2, 2, 64, LAT), BF16),
        ((2, CHUNKS, 512, 128), BF16),
        ((2, CHUNKS, 64, LAT), BF16),
        ((2, 2, 256, 128), BF16),
        ((2, 2, 512, 128), BF16),
        ((2, 2, 32, LAT), BF16),
        ((2, 2, 64, LAT), BF16),
    ]
    results = pl.pallas_call(
        kernel,
        out_shape=(
            jax.ShapeDtypeStruct((ROWS_DEV, WIDTH), BF16),
            jax.ShapeDtypeStruct((128, LAT), F32),
            jax.ShapeDtypeStruct((LAT, 128), F32),
        ),
        in_specs=[any_, any_, any_, vmem, vmem, any_, vmem, any_, vmem],
        out_specs=(vmem, vmem, vmem),
        scratch_shapes=[pltpu.VMEM(shape, dtype) for shape, dtype in scratch]
        + [
            pltpu.SemaphoreType.DMA((N_SEMS,)),
            pltpu.SemaphoreType.DMA((N_SEMS,)),
            pltpu.SemaphoreType.DMA((20,)),
        ],
        compiler_params=pltpu.CompilerParams(
            collective_id=0, has_side_effects=True, vmem_limit_bytes=67043328
        ),
    )(
        queries, cache_keys, cache_values, positions.reshape(1, -1), shuffle.reshape(1, -1),
        enc_weight, enc_bias.reshape(1, -1), dec_weight, dec_bias.reshape(1, -1),
    )
    return pl.pallas_call(
        finish_kernel,
        out_shape=tuple(jax.ShapeDtypeStruct(r.shape, r.dtype) for r in results),
        in_specs=[any_, any_, any_],
        out_specs=(any_, any_, any_),
        scratch_shapes=[pltpu.VMEM(r.shape, r.dtype) for r in results] + [pltpu.SemaphoreType.DMA((2, 3))],
    )(*results)


def solution(mesh):
    in_specs = (
        P(("dp", "latent"), None),
        P(("dp", "latent"), None, None),
        P(("dp", "latent"), None, None),
        P(("dp", "latent")),
        P(("dp", "latent")),
        P(None, "latent"),
        P("latent"),
        P("latent", None),
        P(),
    )
    out_specs = (P(("dp", "latent"), None), P("dp", "latent"), P("latent", "dp"))
    return jax.shard_map(shards, mesh=mesh, in_specs=in_specs, out_specs=out_specs, check_vma=False)
```

```python
import jax
import jax.numpy as jnp
from jax import lax
from jax.experimental import pallas as pl
from jax.experimental.pallas import tpu as pltpu
from jax.sharding import PartitionSpec as P

F32 = jnp.float32
BF16 = jnp.bfloat16
MESH = pl.DeviceIdType.MESH

HEAD_DIM = 256
KV_HEADS = 4
HEADS = 8
CACHE = 512
ROWS_DEV = 32
GROUP = 512
WIDTH = 2048
LAT = 1024
ALL_ROWS = 8192
N_X = 4
N_Z = 8
N_DP = 16
CHUNKS = 4
COLS = WIDTH // CHUNKS
EPSILON = 1e-06
GRAD_SCALE = 2.0 / ALL_ROWS
SPARSE_SCALE = 1.0 / ALL_ROWS

N_SEMS = 300


def dot(a, b):
    return jnp.dot(a, b, preferred_element_type=F32)


def dot_nt(a, b):
    return lax.dot_general(a, b, (((1,), (1,)), ((), ())), preferred_element_type=F32)


def iota(shape, axis):
    return lax.broadcasted_iota(jnp.int32, shape, axis)


def chunk_dp(j, s):
    return s * N_X + (j - s) % N_X


def kernel(
    queries, keys, values, positions, shuffle, enc_w, enc_bias, dec_w, dec_bias,
    rebuilt_out, enc_out, dec_out,
    q_v, k_v, v_v, enc_v, dec_v, heads, outgoing, arrived, notes_out, notes_in,
    energies, gathered, inputs, batch, inputs_t, coded, coded_t, gate, norm_row, dec_coef,
    part_send, part_recv, part_own, rs_send_p, rs_recv_p, rs_send_m, rs_recv_m,
    residual, grad_act, grad_pre, dec_term, enc_term,
    dec_r1, dec_r2, enc_r1, enc_r2, dec_u, enc_u, dec_s1, dec_s2, enc_s1, enc_s2,
    send_sems, recv_sems, local_sems,
):
    me_dp = lax.axis_index("dp")
    me_l = lax.axis_index("latent")
    x, y = me_dp // N_X, me_dp % N_X
    z, core = me_l // 2, me_l % 2
    other = 1 - core

    def at_z(k):
        return {"latent": lax.rem(z + k + N_Z, N_Z) * 2 + core}

    partner = {"latent": z * 2 + other}

    def at_x(k):
        return {"dp": lax.rem(x + k + N_X, N_X) * N_X + y}

    def at_y(k):
        return {"dp": x * N_X + lax.rem(y + k + N_X, N_X)}

    counter = [0]
    sent = []

    def remote(src, dst, device):
        i = counter[0]
        counter[0] += 1
        return pltpu.make_async_remote_copy(
            src_ref=src, dst_ref=dst, send_sem=send_sems.at[i], recv_sem=recv_sems.at[i],
            device_id=device, device_id_type=MESH,
        )

    def start(copy):
        copy.start()
        sent.append(copy)
        return copy

    def load(src, dst, i):
        c = pltpu.make_async_copy(src, dst, local_sems.at[i])
        c.start()
        return c

    load_q = load(queries, q_v, 0)
    load_k = load(keys.at[0], k_v, 1)
    load_v = load(values.at[0], v_v, 2)
    barrier = pltpu.get_barrier_semaphore()
    for o in range(1, N_DP):
        pl.semaphore_signal(barrier, inc=1, device_id={"dp": lax.rem(me_dp + o, N_DP)}, device_id_type=MESH)
        pl.semaphore_signal(barrier, inc=1, device_id={"latent": lax.rem(me_l + o, N_DP)}, device_id_type=MESH)

    shuffle_row = shuffle[...]
    sub = iota((ROWS_DEV, ROWS_DEV), 0)
    lane = iota((ROWS_DEV, ROWS_DEV), 1)
    eye = sub == lane
    wide = jnp.broadcast_to(shuffle_row, (ROWS_DEV, ROWS_DEV))
    shuffle_col = jnp.sum(jnp.where(eye, wide.astype(F32), 0.0), axis=1, keepdims=True).astype(jnp.int32)
    target_row = lax.shift_right_logical(wide, 9)
    target_col = lax.shift_right_logical(shuffle_col, 9)
    before = jnp.where((target_row == target_col) & (lane < sub), 1.0, 0.0)
    slot_col = 2.0 * target_col.astype(F32) + jnp.sum(before, axis=1, keepdims=True)
    lane_w = iota((ROWS_DEV, 256), 1)
    sub_w = iota((ROWS_DEV, 256), 0)
    slot_wide = jnp.sum(
        jnp.where((lane_w & 31) == sub_w, jnp.broadcast_to(slot_col, (ROWS_DEV, 256)), 0.0), axis=0, keepdims=True
    ).astype(jnp.int32)
    slot_row = jnp.sum(jnp.where(eye, jnp.broadcast_to(slot_col, (ROWS_DEV, ROWS_DEV)), 0.0), axis=0, keepdims=True)
    slot_row = slot_row.astype(jnp.int32)
    place_row = (shuffle_row & 31).astype(F32)
    sub_q = iota((256, 256), 0)
    lane_q = iota((256, 256), 1)
    pick = (sub_q & 7) == lax.shift_right_logical(lane_q, 5)
    pick = pick & (lax.shift_right_logical(sub_q, 3) == slot_wide)
    pick = jnp.where(pick, 1.0, 0.0).astype(BF16)

    pos_wide = jnp.broadcast_to(positions[...], (ROWS_DEV, ROWS_DEV)).astype(F32)
    pos_col = jnp.sum(jnp.where(eye, pos_wide, 0.0), axis=1, keepdims=True).astype(jnp.int32)
    pos_col = jnp.concatenate([pos_col, pos_col], axis=0)
    visible = iota((2 * ROWS_DEV, CACHE), 1) <= pos_col
    load_q.wait()
    load_k.wait()
    load_v.wait()
    load_e = load(enc_w, enc_v, 3)
    load_d = []
    for j in range(CHUNKS):
        for s in range(N_X):
            d = chunk_dp(j, s)
            load_d.append(
                load(dec_w.at[:, d * 128:(d + 1) * 128], dec_v.at[j, :, s * 128:(s + 1) * 128], 4 + j * N_X + s)
            )
    energy = jnp.zeros((1, 1), F32)
    for g in range(KV_HEADS):
        cols = slice(g * HEAD_DIM, (g + 1) * HEAD_DIM)
        pair = jnp.concatenate(
            [q_v[:, (2 * g + i) * HEAD_DIM:(2 * g + i + 1) * HEAD_DIM] for i in range(2)], axis=0
        )
        scores = dot_nt(pair, k_v[:, cols]) * HEAD_DIM ** (-0.5)
        scores = jnp.where(visible, scores, -jnp.inf)
        weights = jnp.exp(scores - jnp.max(scores, axis=1, keepdims=True))
        probs = (weights / jnp.sum(weights, axis=1, keepdims=True)).astype(BF16)
        mixed = dot(probs, v_v[:, cols]).astype(BF16)
        heads[g * 64:(g + 1) * 64, :] = mixed
        square = jnp.square(mixed.astype(F32))
        energy = energy + jnp.sum(jnp.sum(square, axis=1, keepdims=True), axis=0, keepdims=True)
    outgoing[...] = dot(pick, heads[...]).astype(BF16)

    note_lane = iota((128, 128), 1)
    peer_sub = lax.shift_right_logical(iota((128, ROWS_DEV), 0), 3)
    slot_n = jnp.broadcast_to(slot_row, (128, ROWS_DEV))
    place_n = jnp.broadcast_to(place_row, (128, ROWS_DEV))
    place = [
        jnp.sum(jnp.where(slot_n == 2 * peer_sub + k, place_n, 0.0), axis=1, keepdims=True) for k in range(2)
    ]
    mine = lax.shift_right_logical(note_lane, 3) == me_dp
    place_note = jnp.where((note_lane & 4) == 0, place[0], place[1])
    place_note = jnp.where((note_lane & 1) == 0, place_note, jnp.broadcast_to(energy, (128, 128)))
    notes_out[...] = jnp.where(mine, place_note, 0.0)

    pl.semaphore_wait(barrier, 2 * (N_DP - 1))
    own16 = pl.ds(pl.multiple_of(me_dp * 16, 16), 16)
    own8 = pl.ds(pl.multiple_of(me_dp * 8, 8), 8)
    waits = []
    for o in range(1, N_DP):
        to = lax.rem(me_dp + o, N_DP)
        frm = lax.rem(me_dp + N_DP - o, N_DP)
        to16 = pl.ds(pl.multiple_of(to * 16, 16), 16)
        to8 = pl.ds(pl.multiple_of(to * 8, 8), 8)
        frm16 = pl.ds(pl.multiple_of(frm * 16, 16), 16)
        frm8 = pl.ds(pl.multiple_of(frm * 8, 8), 8)
        for src, dst, to_at, own_at, frm_at in (
            (outgoing, arrived, to16, own16, frm16),
            (notes_out, notes_in, to8, own8, frm8),
        ):
            i = counter[0]
            c = start(remote(src.at[to_at], dst.at[own_at], {"dp": to}))
            waits.append(
                pltpu.make_async_remote_copy(
                    src_ref=src.at[to_at], dst_ref=dst.at[frm_at], send_sem=send_sems.at[i],
                    recv_sem=recv_sems.at[i], device_id={"dp": to}, device_id_type=MESH,
                )
            )
    arrived[own16, :] = outgoing[own16, :]
    notes_in[own8, :] = notes_out[own8, :]
    for c in load_d:
        c.wait()
    diag = iota((128, 128), 0) == iota((128, 128), 1)
    norms = []
    for b in range(LAT // 128):
        total = jnp.zeros((128, 1), F32)
        for j in range(CHUNKS):
            total = total + jnp.sum(jnp.square(dec_v[j, b * 128:(b + 1) * 128, :].astype(F32)), axis=1, keepdims=True)
        norm = jnp.sqrt(total + EPSILON)
        norms.append(norm)
        norm_row[0:1, b * 128:(b + 1) * 128] = SPARSE_SCALE * jnp.sum(
            jnp.where(diag, jnp.broadcast_to(norm, (128, 128)), 0.0), axis=0, keepdims=True
        )
        dec_coef[b * 128:(b + 1) * 128, :] = jnp.broadcast_to(SPARSE_SCALE / norm, (128, 128))

    for c in waits:
        c.wait_recv()
    note = notes_in[0:8, :]
    for s in range(1, N_DP):
        note = note + notes_in[s * 8:(s + 1) * 8, :]
    from_lane = iota((128, 256), 0)
    to_lane = iota((128, 256), 1)
    spread = lax.shift_right_logical(from_lane, 3) == lax.shift_right_logical(to_lane, 4)
    spread = spread & ((from_lane & 7) == lax.shift_right_logical(to_lane & 8, 1))
    places = jnp.where((iota((8, 128), 1) & 1) == 0, note, 0.0).astype(BF16)
    places = dot(places, jnp.where(spread, 1.0, 0.0).astype(BF16))
    place_q = jnp.broadcast_to(places[0:1, :].astype(jnp.int32), (256, 256))
    column_energy = jnp.sum(jnp.where((iota((8, 128), 1) & 7) == 1, note, 0.0), axis=1, keepdims=True)
    put = lax.shift_right_logical(sub_q, 5) == (lane_q & 7)
    put = put & ((sub_q & 31) == place_q)
    placed = dot(jnp.where(put, 1.0, 0.0).astype(BF16), arrived[...]).astype(BF16)

    def block(zb, cb, offset=0, size=ROWS_DEV):
        return pl.ds(pl.multiple_of((cb * N_Z + zb) * ROWS_DEV + offset, 16), size)

    def chip(k):
        return lax.rem(z + k + N_Z, N_Z)

    own = block(z, core)
    half = ROWS_DEV // 2

    def hop(buf, zb, offset, size, device, arrives):
        ref = buf.at[block(zb, core, offset, size)]
        copy = remote(ref, ref, device)
        got_ref = buf.at[block(arrives, core, offset, size)]
        arrival = same_semaphores(got_ref, device)
        pass_on = remote(got_ref, got_ref, partner)
        passed = same_semaphores(buf.at[block(arrives, other, offset, size)], partner)
        return copy, arrival, pass_on, passed

    def same_semaphores(ref, device):
        i = counter[0] - 1
        return pltpu.make_async_remote_copy(
            src_ref=ref, dst_ref=ref, send_sem=send_sems.at[i], recv_sem=recv_sems.at[i],
            device_id=device, device_id_type=MESH,
        )

    def own_hop(buf):
        pass_on = remote(buf.at[own], buf.at[own], partner)
        return pass_on, same_semaphores(buf.at[block(z, other)], partner)

    def gather(buf, deep):
        near, far, third, fourth = {}, {}, {}, {}
        for sign in (1, -1):
            near[sign] = hop(buf, z, 0, ROWS_DEV, at_z(sign), chip(-sign))
            if deep:
                far[sign] = hop(buf, chip(-sign), 0, ROWS_DEV, at_z(sign), chip(-2 * sign))
            else:
                far[sign] = hop(buf, z, 0, ROWS_DEV, at_z(2 * sign), chip(-2 * sign))
            third[sign] = hop(buf, chip(-2 * sign), 0, ROWS_DEV, at_z(sign), chip(-3 * sign))
            fourth[sign] = hop(buf, chip(-2 * sign), 0 if sign == 1 else half, half, at_z(2 * sign), chip(4))
        own_pass, own_passed = own_hop(buf)
        passed = {0: [own_passed], 4: [fourth[1][3], fourth[-1][3]]}
        for sign in (1, -1):
            for k, group in ((1, near), (2, far), (3, third)):
                passed[-sign * k] = [group[sign][3]]

        def first():
            if not deep:
                for sign in (1, -1):
                    start(far[sign][0])
            for sign in (1, -1):
                start(near[sign][0])
            start(own_pass)

        def relay():
            for sign in (1, -1):
                near[sign][1].wait_recv()
                start(far[sign][0])
                start(near[sign][2])

        def middle():
            for sign in (1, -1):
                far[sign][1].wait_recv()
                start(fourth[sign][0])
                start(third[sign][0])
                start(far[sign][2])
            if not deep:
                for sign in (1, -1):
                    near[sign][1].wait_recv()
                    start(near[sign][2])

        def last():
            for group in (third, fourth):
                for sign in (1, -1):
                    group[sign][1].wait_recv()
                    start(group[sign][2])

        def finish(names=tuple(passed)):
            for name in names:
                for copy in passed[name]:
                    copy.wait_recv()

        return ([first, relay, middle, last] if deep else [first, middle, last]), finish

    for h in range(HEADS):
        gathered[h // 2, own, (h % 2) * 256:(h % 2 + 1) * 256] = placed[h * 32:(h + 1) * 32, :]
    energies[me_l] = jnp.broadcast_to(column_energy, (8, 128))
    e_waits = []
    for o in range(1, N_DP):
        to = lax.rem(me_l + o, N_DP)
        frm = lax.rem(me_l + N_DP - o, N_DP)
        start(remote(energies.at[me_l], energies.at[me_l], {"latent": to}))
        e_waits.append(same_semaphores(energies.at[frm], {"latent": to}))
    rings = [gather(gathered.at[c], True) for c in range(CHUNKS)]

    def step(k):
        for ring in rings:
            ring[0][k]()

    def finish(*names):
        for ring in rings:
            ring[1](names)

    step(0)
    step(1)
    for c in e_waits:
        c.wait_recv()
    total = energies[0]
    for s in range(1, N_DP):
        total = total + energies[s]
    norm_scale = lax.rsqrt(total[0:1, 0:1] / (ALL_ROWS * WIDTH) + EPSILON)

    load_e.wait()

    def encode(chips):
        spots = [block(zb, cb) for zb in chips for cb in range(2)]
        for n, spot in enumerate(spots):
            for c in range(CHUNKS):
                scaled = (gathered[c, spot, :].astype(F32) * norm_scale).astype(BF16)
                inputs[spot, c * COLS:(c + 1) * COLS] = scaled
                batch[n * ROWS_DEV:(n + 1) * ROWS_DEV, c * COLS:(c + 1) * COLS] = scaled

        def tile_step(t, carry):
            at = pl.ds(pl.multiple_of(t * 256, 256), 256)
            pre = 4.0 * (dot(batch[0:len(spots) * ROWS_DEV, :], enc_v[:, at]) + enc_bias[:, at])
            small = jnp.exp(-jnp.abs(pre))
            active = 0.25 * (jnp.maximum(pre, 0.0) + jnp.log1p(small))
            sig = jnp.where(pre >= 0, 1.0, small) / (1.0 + small)
            act = active.astype(BF16)
            for n, spot in enumerate(spots):
                part = slice(n * ROWS_DEV, (n + 1) * ROWS_DEV)
                coded[spot, at] = act[part, :]
                gate[spot, at] = sig[part, :]
            return carry

        lax.fori_loop(0, LAT // 256, tile_step, 0)

    step(2)
    finish(0, -1)
    encode((z, chip(-1)))
    finish(1, 2)
    encode((chip(1), chip(2)))
    step(3)
    finish(-2, 3, -3, 4)
    encode((chip(-2), chip(3), chip(-3), chip(4)))

    events = []

    def at_time(t, fn):
        events.append((t, len(events), fn))

    own_half = pl.ds(pl.multiple_of(core * 256, 256), 256)
    other_half = pl.ds(pl.multiple_of(other * 256, 256), 256)

    def transpose_coded(b):
        def run():
            turned = coded[:, b * 256:(b + 1) * 256].T
            coded_t[b * 256:(b + 1) * 256, :] = turned
            sums = jnp.sum(turned.astype(F32), axis=1, keepdims=True)
            dec_coef[b * 256:(b + 1) * 256, :] = dec_coef[b * 256:(b + 1) * 256, :] * sums
        return run

    def transpose_inputs(j):
        def run():
            for s in range(N_X):
                d = chunk_dp(j, s)
                inputs_t[j, s * 128:(s + 1) * 128, :] = inputs[:, d * 128:(d + 1) * 128].T
        return run

    for b in range(4):
        at_time((2.5, 6.6, 6.7, 9.1)[b], transpose_coded(b))
        at_time((11.1, 13.3, 15.6, 17.1)[b], transpose_inputs(b))

    def latent_stream(j):
        deep = j >= 2
        begin = (0.0, 1.0, 3.8, 4.8)[j]
        times = (
            (2.2, 6.0, 10.2, 14.4, 18.2, 19.4),
            (3.6, 8.5, 13.0, 18.0, 22.5, 24.0),
            (5.0, 9.0, 13.2, 17.0, 20.5, 24.2, 27.5, 29.0),
            (6.5, 11.0, 15.5, 20.0, 23.5, 27.6, 31.5, 33.0),
        )[j]
        swap = remote(part_send.at[j], part_recv.at[j], partner)

        def start_half():
            part_send[j] = dot(coded[other_half, :], dec_v[j]).astype(BF16)
            start(swap)

        def own_part():
            part_own[j] = dot(coded[own_half, :], dec_v[j])

        sides = ((1, rs_send_p, rs_recv_p), (-1, rs_send_m, rs_recv_m))
        hops = {}
        for sign, out_buf, in_buf in sides:
            near = slice(0, 16) if sign == 1 else slice(16, 32)
            for slot, dist in ((0, 2), (1, 1), (2, 1 if deep else 2), (3, 1)):
                rows = near if slot == 0 else slice(0, 32)
                hops[(sign, slot)] = remote(out_buf.at[j, slot, rows], in_buf.at[j, slot, rows], at_z(dist * sign))

        def own_block(zb):
            rows = pl.ds(pl.multiple_of(zb * ROWS_DEV, ROWS_DEV), ROWS_DEV)
            return part_own[j, rows, :] + part_recv[j, rows, :].astype(F32)

        def reduce_first():
            swap.wait_recv()
            for slot, dist in ((0, 4), (1, 3)) if deep else ((0, 4), (1, 3), (3, 1)):
                for sign, out_buf, in_buf in sides:
                    mine_ = own_block(chip(sign * dist))
                    near = slice(0, 16) if sign == 1 else slice(16, 32)
                    rows = near if slot == 0 else slice(0, 32)
                    out_buf[j, slot, rows, :] = mine_[rows, :].astype(BF16)
                    start(hops[(sign, slot)])

        def reduce_second():
            for sign, out_buf, in_buf in sides:
                near = slice(0, 16) if sign == 1 else slice(16, 32)
                far = slice(16, 32) if sign == 1 else slice(0, 16)
                hops[(sign, 1)].wait_recv()
                hops[(sign, 0)].wait_recv()
                mine_ = own_block(chip(sign * 2)) + in_buf[j, 1, :, :].astype(F32)
                out_buf[j, 2, near, :] = (mine_[near, :] + in_buf[j, 0, near, :].astype(F32)).astype(BF16)
                out_buf[j, 2, far, :] = mine_[far, :].astype(BF16)
                start(hops[(sign, 2)])

        def reduce_third():
            for sign, out_buf, in_buf in sides:
                hops[(sign, 2)].wait_recv()
                out_buf[j, 3, :, :] = (own_block(chip(sign)) + in_buf[j, 2, :, :].astype(F32)).astype(BF16)
                start(hops[(sign, 3)])

        spread_steps, finish_ = gather(residual.at[j], deep)

        def own_sum():
            summed = own_block(z)
            for slot in (3,) if deep else (3, 2):
                for sign, out_buf, in_buf in sides:
                    hops[(sign, slot)].wait_recv()
                    summed = summed + in_buf[j, slot, :, :].astype(F32)
            spans = [slice(chunk_dp(j, s) * 128, chunk_dp(j, s) * 128 + 128) for s in range(N_X)]
            bias = jnp.concatenate([dec_bias[:, sp] for sp in spans], axis=1)
            rebuilt = summed + bias
            rebuilt_half = rebuilt.astype(BF16)
            for s, sp in enumerate(spans):
                rebuilt_out[:, sp] = rebuilt_half[:, s * 128:(s + 1) * 128]
            ins = jnp.concatenate([inputs[own, sp] for sp in spans], axis=1).astype(F32)
            residual[j, own, :] = (rebuilt - ins).astype(BF16)
            spread_steps[0]()

        steps = [reduce_first, reduce_second] + ([reduce_third] if deep else []) + [own_sum] + spread_steps[1:]
        at_time(begin, start_half)
        at_time(begin + 0.5, own_part)
        for step_at, fn in zip(times, steps):
            at_time(step_at, fn)
        return times[-1], finish_

    def pair_reduce(pick_ref, split, first_in, second_in, hop, me):
        a, b = (0, split), (split, split)
        far = lax.rem(me + 2, N_X)
        up, down = lax.rem(me + 1, N_X), lax.rem(me + 3, N_X)
        full = (0, 2 * split)
        far_up = remote(pick_ref(far, a), first_in.at[0], hop(1))
        far_down = remote(pick_ref(far, b), first_in.at[1], hop(-1))
        near_up = remote(pick_ref(up, full), second_in.at[0], hop(1))
        near_down = remote(pick_ref(down, full), second_in.at[1], hop(-1))

        def go():
            start(far_up)
            start(far_down)

        def combine():
            for copy, place_, part, ref, nxt in (
                (far_up, up, a, first_in.at[0], near_up),
                (far_down, down, b, first_in.at[1], near_down),
            ):
                copy.wait_recv()
                spot = pick_ref(place_, part)
                spot[...] = (spot[...].astype(F32) + ref[...].astype(F32)).astype(BF16)
                start(nxt)

        def total():
            near_up.wait_recv()
            near_down.wait_recv()
            spot = pick_ref(me, full)
            return spot[...].astype(F32) + second_in[0].astype(F32) + second_in[1].astype(F32)

        return go, combine, total

    def grad_stream(term, halves, r1, r2, u, s1, s2, out, rows):
        half = rows // 2
        split = half // 2
        parts = []
        for j in range(CHUNKS):
            both = []
            for o in range(2):
                me = x if o == 0 else y
                hop = at_x if o == 0 else at_y

                def pick_ref(i, part, j=j, o=o):
                    s = i if o == 0 else lax.rem(j - i + N_X, N_X)
                    return term.at[j, s, pl.ds(o * half + part[0], part[1])]

                both.append(pair_reduce(pick_ref, split, r1.at[j, o], r2.at[j, o], hop, me))
            parts.append(both)
        tail = []
        for o in range(2):
            me = y if o == 0 else x
            hop = at_y if o == 0 else at_x

            def pick_ref(i, part, o=o):
                j = lax.rem(i + (x if o == 0 else y), N_X)
                return u.at[o, j, pl.ds(part[0], part[1])]

            tail.append(pair_reduce(pick_ref, split, s1.at[o], s2.at[o], hop, me))

        def fold(j):
            def run():
                for o in range(2):
                    u[o, j] = parts[j][o][2]().astype(BF16)
            return run

        def go(j):
            for o in range(2):
                parts[j][o][0]()

        def combine(j):
            def run():
                for o in range(2):
                    parts[j][o][1]()
            return run

        def tail_go():
            for o in range(2):
                tail[o][0]()

        def tail_combine():
            for o in range(2):
                tail[o][1]()

        def tail_total():
            for o in range(2):
                out[o * half:(o + 1) * half, :] = tail[o][2]()

        return go, combine, fold, tail_go, tail_combine, tail_total

    dec_go, dec_combine, dec_fold, dec_tail_go, dec_tail_combine, dec_tail_total = grad_stream(
        dec_term, None, dec_r1, dec_r2, dec_u, dec_s1, dec_s2, dec_out, LAT
    )
    enc_go, enc_combine, enc_fold, enc_tail_go, enc_tail_combine, enc_tail_total = grad_stream(
        enc_term, None, enc_r1, enc_r2, enc_u, enc_s1, enc_s2, enc_out, 128
    )

    def dec_grad(j):
        def run():
            def tile_step(t, carry):
                at = pl.ds(pl.multiple_of(t * 256, 256), 256)
                term = GRAD_SCALE * dot(coded_t[at, :], residual[j])
                coef = dec_coef[at, :]
                for s in range(N_X):
                    sp = slice(s * 128, (s + 1) * 128)
                    dec_term[j, s, at, :] = (term[:, sp] + coef * dec_v[j, at, sp].astype(F32)).astype(BF16)
                return carry

            lax.fori_loop(0, LAT // 256, tile_step, 0)
            dec_go(j)
        return run

    def act_grad(j):
        def run():
            def tile_step(t, carry):
                at = pl.ds(pl.multiple_of(t * 256, 256), 256)
                part = dot_nt(residual[j], dec_v[j, at, :])
                if j == 0:
                    grad_act[:, at] = part
                elif j < CHUNKS - 1:
                    grad_act[:, at] = grad_act[:, at] + part
                else:
                    whole = GRAD_SCALE * (grad_act[:, at] + part) + norm_row[0:1, at]
                    grad_pre[:, at] = (whole * gate[:, at]).astype(BF16)
                return carry

            lax.fori_loop(0, LAT // 256, tile_step, 0)
        return run

    def enc_grad(j):
        def run():
            def tile_step(t, carry):
                at = pl.ds(pl.multiple_of(t * 256, 256), 256)
                term = dot(inputs_t[j], grad_pre[:, at]).astype(BF16)
                for s in range(N_X):
                    enc_term[j, s, :, at] = term[s * 128:(s + 1) * 128, :]
                return carry

            lax.fori_loop(0, LAT // 256, tile_step, 0)
            enc_go(j)
        return run

    WIRE = 4.2
    ready = 0.0
    for j in range(CHUNKS):
        t, all_in = latent_stream(j)
        ready = t
        at_time(ready, all_in)
        at_time(ready + 0.1, dec_grad(j))
        at_time(ready + 0.2, act_grad(j))
        at_time(ready + 4.5, dec_combine(j))
        at_time(ready + 9.0, dec_fold(j))
    dec_end = ready + 9.0
    enc_start = ready + 2.0
    for j in range(CHUNKS):
        t = enc_start + 1.0 * j
        at_time(t, enc_grad(j))
        at_time(t + 5.0 + (WIRE - 1.0) * j, enc_combine(j))
        at_time(t + 9.5 + (WIRE - 1.0) * j, enc_fold(j))
    enc_end = enc_start + 9.5 + WIRE * 3
    at_time(dec_end + 0.1, dec_tail_go)
    at_time(dec_end + 5.0, dec_tail_combine)
    at_time(dec_end + 12.0, dec_tail_total)
    at_time(enc_end + 0.1, enc_tail_go)
    at_time(enc_end + 3.5, enc_tail_combine)
    at_time(enc_end + 8.0, enc_tail_total)

    for _, _, fn in sorted(events, key=lambda e: (e[0], e[1])):
        fn()
    for copy in sent:
        copy.wait_send()


def finish_kernel(*refs):
    ins, outs, bufs, sems = refs[0:3], refs[3:6], refs[6:9], refs[9]
    loads = [pltpu.make_async_copy(a, b, sems.at[0, i]) for i, (a, b) in enumerate(zip(ins, bufs))]
    stores = [pltpu.make_async_copy(a, b, sems.at[1, i]) for i, (a, b) in enumerate(zip(bufs, outs))]
    for c in loads:
        c.start()
    for a, b in zip(loads, stores):
        a.wait()
        b.start()
    for c in stores:
        c.wait()


def shards(
    queries, cache_keys, cache_values, positions, shuffle, enc_weight, enc_bias, dec_weight, dec_bias
):
    any_ = pl.BlockSpec(memory_space=pl.ANY)
    vmem = pl.BlockSpec(memory_space=pltpu.VMEM)
    scratch = [
        ((ROWS_DEV, WIDTH), BF16),
        ((CACHE, KV_HEADS * HEAD_DIM), BF16),
        ((CACHE, KV_HEADS * HEAD_DIM), BF16),
        ((WIDTH, LAT), BF16),
        ((CHUNKS, LAT, COLS), BF16),
        ((256, 256), BF16),
        ((256, 256), BF16),
        ((256, 256), BF16),
        ((128, 128), F32),
        ((128, 128), F32),
        ((16, 8, 128), F32),
        ((CHUNKS, GROUP, COLS), BF16),
        ((GROUP, WIDTH), BF16),
        ((256, WIDTH), BF16),
        ((CHUNKS, COLS, GROUP), BF16),
        ((GROUP, LAT), BF16),
        ((LAT, GROUP), BF16),
        ((GROUP, LAT), F32),
        ((8, LAT), F32),
        ((LAT, 128), F32),
        ((CHUNKS, 256, COLS), BF16),
        ((CHUNKS, 256, COLS), BF16),
        ((CHUNKS, 256, COLS), F32),
        ((CHUNKS, 4, ROWS_DEV, COLS), BF16),
        ((CHUNKS, 4, ROWS_DEV, COLS), BF16),
        ((CHUNKS, 4, ROWS_DEV, COLS), BF16),
        ((CHUNKS, 4, ROWS_DEV, COLS), BF16),
        ((CHUNKS, GROUP, COLS), BF16),
        ((GROUP, LAT), F32),
        ((GROUP, LAT), BF16),
        ((CHUNKS, 4, LAT, 128), BF16),
        ((CHUNKS, 4, 128, LAT), BF16),
        ((CHUNKS, 2, 2, 256, 128), BF16),
        ((CHUNKS, 2, 2, 512, 128), BF16),
        ((CHUNKS, 2, 2, 32, LAT), BF16),
        ((CHUNKS, 2, 2, 64, LAT), BF16),
        ((2, CHUNKS, 512, 128), BF16),
        ((2, CHUNKS, 64, LAT), BF16),
        ((2, 2, 256, 128), BF16),
        ((2, 2, 512, 128), BF16),
        ((2, 2, 32, LAT), BF16),
        ((2, 2, 64, LAT), BF16),
    ]
    results = pl.pallas_call(
        kernel,
        out_shape=(
            jax.ShapeDtypeStruct((ROWS_DEV, WIDTH), BF16),
            jax.ShapeDtypeStruct((128, LAT), F32),
            jax.ShapeDtypeStruct((LAT, 128), F32),
        ),
        in_specs=[any_, any_, any_, vmem, vmem, any_, vmem, any_, vmem],
        out_specs=(vmem, vmem, vmem),
        scratch_shapes=[pltpu.VMEM(shape, dtype) for shape, dtype in scratch]
        + [
            pltpu.SemaphoreType.DMA((N_SEMS,)),
            pltpu.SemaphoreType.DMA((N_SEMS,)),
            pltpu.SemaphoreType.DMA((20,)),
        ],
        compiler_params=pltpu.CompilerParams(
            collective_id=0, has_side_effects=True, vmem_limit_bytes=67043328
        ),
    )(
        queries, cache_keys, cache_values, positions.reshape(1, -1), shuffle.reshape(1, -1),
        enc_weight, enc_bias.reshape(1, -1), dec_weight, dec_bias.reshape(1, -1),
    )
    return pl.pallas_call(
        finish_kernel,
        out_shape=tuple(jax.ShapeDtypeStruct(r.shape, r.dtype) for r in results),
        in_specs=[any_, any_, any_],
        out_specs=(any_, any_, any_),
        scratch_shapes=[pltpu.VMEM(r.shape, r.dtype) for r in results] + [pltpu.SemaphoreType.DMA((2, 3))],
    )(*results)


def solution(mesh):
    in_specs = (
        P(("dp", "latent"), None),
        P(("dp", "latent"), None, None),
        P(("dp", "latent"), None, None),
        P(("dp", "latent")),
        P(("dp", "latent")),
        P(None, "latent"),
        P("latent"),
        P("latent", None),
        P(),
    )
    out_specs = (P(("dp", "latent"), None), P("dp", "latent"), P("latent", "dp"))
    return jax.shard_map(shards, mesh=mesh, in_specs=in_specs, out_specs=out_specs, check_vma=False)
```

```python
import jax
import jax.numpy as jnp
from jax import lax
from jax.experimental import pallas as pl
from jax.experimental.pallas import tpu as pltpu
from jax.sharding import PartitionSpec as P

F32 = jnp.float32
BF16 = jnp.bfloat16
MESH = pl.DeviceIdType.MESH

HEAD_DIM = 256
KV_HEADS = 4
HEADS = 8
CACHE = 512
ROWS_DEV = 32
GROUP = 512
WIDTH = 2048
LAT = 1024
ALL_ROWS = 8192
N_X = 4
N_Z = 8
N_DP = 16
CHUNKS = 4
COLS = WIDTH // CHUNKS
EPSILON = 1e-06
GRAD_SCALE = 2.0 / ALL_ROWS
SPARSE_SCALE = 1.0 / ALL_ROWS

N_SEMS = 300


def dot(a, b):
    return jnp.dot(a, b, preferred_element_type=F32)


def dot_nt(a, b):
    return lax.dot_general(a, b, (((1,), (1,)), ((), ())), preferred_element_type=F32)


def iota(shape, axis):
    return lax.broadcasted_iota(jnp.int32, shape, axis)


def chunk_dp(j, s):
    return s * N_X + (j - s) % N_X


def kernel(
    queries, keys, values, positions, shuffle, enc_w, enc_bias, dec_w, dec_bias,
    rebuilt_out, enc_out, dec_out,
    q_v, k_v, v_v, enc_v, dec_v, heads, outgoing, arrived, notes_out, notes_in,
    energies, gathered, inputs, batch, inputs_t, coded, coded_t, gate, norm_row, dec_coef,
    part_send, part_recv, part_own, rs_send_p, rs_recv_p, rs_send_m, rs_recv_m,
    residual, grad_act, grad_pre, dec_term, enc_term,
    dec_r1, dec_r2, enc_r1, enc_r2, dec_u, enc_u, dec_s1, dec_s2, enc_s,
    send_sems, recv_sems, local_sems,
):
    me_dp = lax.axis_index("dp")
    me_l = lax.axis_index("latent")
    x, y = me_dp // N_X, me_dp % N_X
    z, core = me_l // 2, me_l % 2
    other = 1 - core

    def at_z(k):
        return {"latent": lax.rem(z + k + N_Z, N_Z) * 2 + core}

    partner = {"latent": z * 2 + other}

    def at_x(k):
        return {"dp": lax.rem(x + k + N_X, N_X) * N_X + y}

    def at_y(k):
        return {"dp": x * N_X + lax.rem(y + k + N_X, N_X)}

    counter = [0]
    sent = []

    def remote(src, dst, device):
        i = counter[0]
        counter[0] += 1
        return pltpu.make_async_remote_copy(
            src_ref=src, dst_ref=dst, send_sem=send_sems.at[i], recv_sem=recv_sems.at[i],
            device_id=device, device_id_type=MESH,
        )

    def start(copy):
        copy.start()
        sent.append(copy)
        return copy

    def load(src, dst, i):
        c = pltpu.make_async_copy(src, dst, local_sems.at[i])
        c.start()
        return c

    load_q = load(queries, q_v, 0)
    load_k = load(keys.at[0], k_v, 1)
    load_v = load(values.at[0], v_v, 2)
    barrier = pltpu.get_barrier_semaphore()
    for o in range(1, N_DP):
        pl.semaphore_signal(barrier, inc=1, device_id={"dp": lax.rem(me_dp + o, N_DP)}, device_id_type=MESH)
        pl.semaphore_signal(barrier, inc=1, device_id={"latent": lax.rem(me_l + o, N_DP)}, device_id_type=MESH)

    shuffle_row = shuffle[...]
    sub = iota((ROWS_DEV, ROWS_DEV), 0)
    lane = iota((ROWS_DEV, ROWS_DEV), 1)
    eye = sub == lane
    wide = jnp.broadcast_to(shuffle_row, (ROWS_DEV, ROWS_DEV))
    shuffle_col = jnp.sum(jnp.where(eye, wide.astype(F32), 0.0), axis=1, keepdims=True).astype(jnp.int32)
    target_row = lax.shift_right_logical(wide, 9)
    target_col = lax.shift_right_logical(shuffle_col, 9)
    before = jnp.where((target_row == target_col) & (lane < sub), 1.0, 0.0)
    slot_col = 2.0 * target_col.astype(F32) + jnp.sum(before, axis=1, keepdims=True)
    lane_w = iota((ROWS_DEV, 256), 1)
    sub_w = iota((ROWS_DEV, 256), 0)
    slot_wide = jnp.sum(
        jnp.where((lane_w & 31) == sub_w, jnp.broadcast_to(slot_col, (ROWS_DEV, 256)), 0.0), axis=0, keepdims=True
    ).astype(jnp.int32)
    slot_row = jnp.sum(jnp.where(eye, jnp.broadcast_to(slot_col, (ROWS_DEV, ROWS_DEV)), 0.0), axis=0, keepdims=True)
    slot_row = slot_row.astype(jnp.int32)
    place_row = (shuffle_row & 31).astype(F32)
    sub_q = iota((256, 256), 0)
    lane_q = iota((256, 256), 1)
    pick = (sub_q & 7) == lax.shift_right_logical(lane_q, 5)
    pick = pick & (lax.shift_right_logical(sub_q, 3) == slot_wide)
    pick = jnp.where(pick, 1.0, 0.0).astype(BF16)

    pos_wide = jnp.broadcast_to(positions[...], (ROWS_DEV, ROWS_DEV)).astype(F32)
    pos_col = jnp.sum(jnp.where(eye, pos_wide, 0.0), axis=1, keepdims=True).astype(jnp.int32)
    pos_col = jnp.concatenate([pos_col, pos_col], axis=0)
    visible = iota((2 * ROWS_DEV, CACHE), 1) <= pos_col
    load_q.wait()
    load_k.wait()
    load_v.wait()
    load_e = load(enc_w, enc_v, 3)
    load_d = []
    for j in range(CHUNKS):
        for s in range(N_X):
            d = chunk_dp(j, s)
            load_d.append(
                load(dec_w.at[:, d * 128:(d + 1) * 128], dec_v.at[j, :, s * 128:(s + 1) * 128], 4 + j * N_X + s)
            )
    energy = jnp.zeros((1, 1), F32)
    for g in range(KV_HEADS):
        cols = slice(g * HEAD_DIM, (g + 1) * HEAD_DIM)
        pair = jnp.concatenate(
            [q_v[:, (2 * g + i) * HEAD_DIM:(2 * g + i + 1) * HEAD_DIM] for i in range(2)], axis=0
        )
        scores = dot_nt(pair, k_v[:, cols]) * HEAD_DIM ** (-0.5)
        scores = jnp.where(visible, scores, -jnp.inf)
        weights = jnp.exp(scores - jnp.max(scores, axis=1, keepdims=True))
        probs = (weights / jnp.sum(weights, axis=1, keepdims=True)).astype(BF16)
        mixed = dot(probs, v_v[:, cols]).astype(BF16)
        heads[g * 64:(g + 1) * 64, :] = mixed
        square = jnp.square(mixed.astype(F32))
        energy = energy + jnp.sum(jnp.sum(square, axis=1, keepdims=True), axis=0, keepdims=True)
    outgoing[...] = dot(pick, heads[...]).astype(BF16)

    note_lane = iota((128, 128), 1)
    peer_sub = lax.shift_right_logical(iota((128, ROWS_DEV), 0), 3)
    slot_n = jnp.broadcast_to(slot_row, (128, ROWS_DEV))
    place_n = jnp.broadcast_to(place_row, (128, ROWS_DEV))
    place = [
        jnp.sum(jnp.where(slot_n == 2 * peer_sub + k, place_n, 0.0), axis=1, keepdims=True) for k in range(2)
    ]
    mine = lax.shift_right_logical(note_lane, 3) == me_dp
    place_note = jnp.where((note_lane & 4) == 0, place[0], place[1])
    place_note = jnp.where((note_lane & 1) == 0, place_note, jnp.broadcast_to(energy, (128, 128)))
    notes_out[...] = jnp.where(mine, place_note, 0.0)

    pl.semaphore_wait(barrier, 2 * (N_DP - 1))
    own16 = pl.ds(pl.multiple_of(me_dp * 16, 16), 16)
    own8 = pl.ds(pl.multiple_of(me_dp * 8, 8), 8)
    waits = []
    for o in range(1, N_DP):
        to = lax.rem(me_dp + o, N_DP)
        frm = lax.rem(me_dp + N_DP - o, N_DP)
        to16 = pl.ds(pl.multiple_of(to * 16, 16), 16)
        to8 = pl.ds(pl.multiple_of(to * 8, 8), 8)
        frm16 = pl.ds(pl.multiple_of(frm * 16, 16), 16)
        frm8 = pl.ds(pl.multiple_of(frm * 8, 8), 8)
        for src, dst, to_at, own_at, frm_at in (
            (outgoing, arrived, to16, own16, frm16),
            (notes_out, notes_in, to8, own8, frm8),
        ):
            i = counter[0]
            c = start(remote(src.at[to_at], dst.at[own_at], {"dp": to}))
            waits.append(
                pltpu.make_async_remote_copy(
                    src_ref=src.at[to_at], dst_ref=dst.at[frm_at], send_sem=send_sems.at[i],
                    recv_sem=recv_sems.at[i], device_id={"dp": to}, device_id_type=MESH,
                )
            )
    arrived[own16, :] = outgoing[own16, :]
    notes_in[own8, :] = notes_out[own8, :]
    for c in load_d:
        c.wait()
    diag = iota((128, 128), 0) == iota((128, 128), 1)
    norms = []
    for b in range(LAT // 128):
        total = jnp.zeros((128, 1), F32)
        for j in range(CHUNKS):
            total = total + jnp.sum(jnp.square(dec_v[j, b * 128:(b + 1) * 128, :].astype(F32)), axis=1, keepdims=True)
        norm = jnp.sqrt(total + EPSILON)
        norms.append(norm)
        norm_row[0:1, b * 128:(b + 1) * 128] = SPARSE_SCALE * jnp.sum(
            jnp.where(diag, jnp.broadcast_to(norm, (128, 128)), 0.0), axis=0, keepdims=True
        )
        dec_coef[b * 128:(b + 1) * 128, :] = jnp.broadcast_to(SPARSE_SCALE / norm, (128, 128))

    for c in waits:
        c.wait_recv()
    note = notes_in[0:8, :]
    for s in range(1, N_DP):
        note = note + notes_in[s * 8:(s + 1) * 8, :]
    from_lane = iota((128, 256), 0)
    to_lane = iota((128, 256), 1)
    spread = lax.shift_right_logical(from_lane, 3) == lax.shift_right_logical(to_lane, 4)
    spread = spread & ((from_lane & 7) == lax.shift_right_logical(to_lane & 8, 1))
    places = jnp.where((iota((8, 128), 1) & 1) == 0, note, 0.0).astype(BF16)
    places = dot(places, jnp.where(spread, 1.0, 0.0).astype(BF16))
    place_q = jnp.broadcast_to(places[0:1, :].astype(jnp.int32), (256, 256))
    column_energy = jnp.sum(jnp.where((iota((8, 128), 1) & 7) == 1, note, 0.0), axis=1, keepdims=True)
    put = lax.shift_right_logical(sub_q, 5) == (lane_q & 7)
    put = put & ((sub_q & 31) == place_q)
    placed = dot(jnp.where(put, 1.0, 0.0).astype(BF16), arrived[...]).astype(BF16)

    def block(zb, cb, offset=0, size=ROWS_DEV):
        return pl.ds(pl.multiple_of((cb * N_Z + zb) * ROWS_DEV + offset, 16), size)

    def chip(k):
        return lax.rem(z + k + N_Z, N_Z)

    own = block(z, core)
    half = ROWS_DEV // 2

    def hop(buf, zb, offset, size, device, arrives):
        ref = buf.at[block(zb, core, offset, size)]
        copy = remote(ref, ref, device)
        got_ref = buf.at[block(arrives, core, offset, size)]
        arrival = same_semaphores(got_ref, device)
        pass_on = remote(got_ref, got_ref, partner)
        passed = same_semaphores(buf.at[block(arrives, other, offset, size)], partner)
        return copy, arrival, pass_on, passed

    def same_semaphores(ref, device):
        i = counter[0] - 1
        return pltpu.make_async_remote_copy(
            src_ref=ref, dst_ref=ref, send_sem=send_sems.at[i], recv_sem=recv_sems.at[i],
            device_id=device, device_id_type=MESH,
        )

    def own_hop(buf):
        pass_on = remote(buf.at[own], buf.at[own], partner)
        return pass_on, same_semaphores(buf.at[block(z, other)], partner)

    def gather(buf, deep):
        near, far, third, fourth = {}, {}, {}, {}
        for sign in (1, -1):
            near[sign] = hop(buf, z, 0, ROWS_DEV, at_z(sign), chip(-sign))
            if deep:
                far[sign] = hop(buf, chip(-sign), 0, ROWS_DEV, at_z(sign), chip(-2 * sign))
            else:
                far[sign] = hop(buf, z, 0, ROWS_DEV, at_z(2 * sign), chip(-2 * sign))
            third[sign] = hop(buf, chip(-2 * sign), 0, ROWS_DEV, at_z(sign), chip(-3 * sign))
            fourth[sign] = hop(buf, chip(-2 * sign), 0 if sign == 1 else half, half, at_z(2 * sign), chip(4))
        own_pass, own_passed = own_hop(buf)
        passed = {0: [own_passed], 4: [fourth[1][3], fourth[-1][3]]}
        for sign in (1, -1):
            for k, group in ((1, near), (2, far), (3, third)):
                passed[-sign * k] = [group[sign][3]]

        def first():
            if not deep:
                for sign in (1, -1):
                    start(far[sign][0])
            for sign in (1, -1):
                start(near[sign][0])
            start(own_pass)

        def relay():
            for sign in (1, -1):
                near[sign][1].wait_recv()
                start(far[sign][0])
                start(near[sign][2])

        def middle():
            for sign in (1, -1):
                far[sign][1].wait_recv()
                start(fourth[sign][0])
                start(third[sign][0])
                start(far[sign][2])
            if not deep:
                for sign in (1, -1):
                    near[sign][1].wait_recv()
                    start(near[sign][2])

        def last():
            for group in (third, fourth):
                for sign in (1, -1):
                    group[sign][1].wait_recv()
                    start(group[sign][2])

        def finish(names=tuple(passed)):
            for name in names:
                for copy in passed[name]:
                    copy.wait_recv()

        return ([first, relay, middle, last] if deep else [first, middle, last]), finish

    for h in range(HEADS):
        gathered[h // 2, own, (h % 2) * 256:(h % 2 + 1) * 256] = placed[h * 32:(h + 1) * 32, :]
    energies[me_l] = jnp.broadcast_to(column_energy, (8, 128))
    e_waits = []
    for o in range(1, N_DP):
        to = lax.rem(me_l + o, N_DP)
        frm = lax.rem(me_l + N_DP - o, N_DP)
        start(remote(energies.at[me_l], energies.at[me_l], {"latent": to}))
        e_waits.append(same_semaphores(energies.at[frm], {"latent": to}))
    rings = [gather(gathered.at[c], True) for c in range(CHUNKS)]

    def step(k):
        for ring in rings:
            ring[0][k]()

    def finish(*names):
        for ring in rings:
            ring[1](names)

    step(0)
    step(1)
    for c in e_waits:
        c.wait_recv()
    total = energies[0]
    for s in range(1, N_DP):
        total = total + energies[s]
    norm_scale = lax.rsqrt(total[0:1, 0:1] / (ALL_ROWS * WIDTH) + EPSILON)

    load_e.wait()

    def encode(chips):
        spots = [block(zb, cb) for zb in chips for cb in range(2)]
        for n, spot in enumerate(spots):
            for c in range(CHUNKS):
                scaled = (gathered[c, spot, :].astype(F32) * norm_scale).astype(BF16)
                inputs[spot, c * COLS:(c + 1) * COLS] = scaled
                batch[n * ROWS_DEV:(n + 1) * ROWS_DEV, c * COLS:(c + 1) * COLS] = scaled

        def tile_step(t, carry):
            at = pl.ds(pl.multiple_of(t * 256, 256), 256)
            pre = 4.0 * (dot(batch[0:len(spots) * ROWS_DEV, :], enc_v[:, at]) + enc_bias[:, at])
            small = jnp.exp(-jnp.abs(pre))
            active = 0.25 * (jnp.maximum(pre, 0.0) + jnp.log1p(small))
            sig = jnp.where(pre >= 0, 1.0, small) / (1.0 + small)
            act = active.astype(BF16)
            for n, spot in enumerate(spots):
                part = slice(n * ROWS_DEV, (n + 1) * ROWS_DEV)
                coded[spot, at] = act[part, :]
                gate[spot, at] = sig[part, :]
            return carry

        lax.fori_loop(0, LAT // 256, tile_step, 0)

    step(2)
    finish(0, -1)
    encode((z, chip(-1)))
    finish(1, 2)
    encode((chip(1), chip(2)))
    step(3)
    finish(-2, 3, -3, 4)
    encode((chip(-2), chip(3), chip(-3), chip(4)))

    events = []

    def at_time(t, fn):
        events.append((t, len(events), fn))

    own_half = pl.ds(pl.multiple_of(core * 256, 256), 256)
    other_half = pl.ds(pl.multiple_of(other * 256, 256), 256)

    def transpose_coded(b):
        def run():
            turned = coded[:, b * 256:(b + 1) * 256].T
            coded_t[b * 256:(b + 1) * 256, :] = turned
            sums = jnp.sum(turned.astype(F32), axis=1, keepdims=True)
            dec_coef[b * 256:(b + 1) * 256, :] = dec_coef[b * 256:(b + 1) * 256, :] * sums
        return run

    def transpose_inputs(j):
        def run():
            for s in range(N_X):
                d = chunk_dp(j, s)
                inputs_t[j, s * 128:(s + 1) * 128, :] = inputs[:, d * 128:(d + 1) * 128].T
        return run

    for b in range(4):
        at_time((2.5, 6.6, 6.7, 9.1)[b], transpose_coded(b))
        at_time((11.1, 13.3, 15.6, 17.1)[b], transpose_inputs(b))

    def latent_stream(j):
        deep = j >= 9
        begin = (0.0, 1.0, 3.0, 7.0)[j]
        times = (
            (2.2, 6.0, 10.2, 14.4, 18.2, 19.4),
            (3.6, 8.5, 13.0, 18.0, 22.5, 24.0),
            (8.4, 12.4, 16.6, 21.0, 25.2, 26.6),
            (12.8, 16.8, 21.0, 25.4, 29.6, 31.0),
        )[j]
        swap = remote(part_send.at[j], part_recv.at[j], partner)

        def start_half():
            part_send[j] = dot(coded[other_half, :], dec_v[j]).astype(BF16)
            start(swap)

        def own_part():
            part_own[j] = dot(coded[own_half, :], dec_v[j])

        sides = ((1, rs_send_p, rs_recv_p), (-1, rs_send_m, rs_recv_m))
        hops = {}
        for sign, out_buf, in_buf in sides:
            near = slice(0, 16) if sign == 1 else slice(16, 32)
            for slot, dist in ((0, 2), (1, 1), (2, 1 if deep else 2), (3, 1)):
                rows = near if slot == 0 else slice(0, 32)
                hops[(sign, slot)] = remote(out_buf.at[j, slot, rows], in_buf.at[j, slot, rows], at_z(dist * sign))

        def own_block(zb):
            rows = pl.ds(pl.multiple_of(zb * ROWS_DEV, ROWS_DEV), ROWS_DEV)
            return part_own[j, rows, :] + part_recv[j, rows, :].astype(F32)

        def reduce_first():
            swap.wait_recv()
            for slot, dist in ((0, 4), (1, 3)) if deep else ((0, 4), (1, 3), (3, 1)):
                for sign, out_buf, in_buf in sides:
                    mine_ = own_block(chip(sign * dist))
                    near = slice(0, 16) if sign == 1 else slice(16, 32)
                    rows = near if slot == 0 else slice(0, 32)
                    out_buf[j, slot, rows, :] = mine_[rows, :].astype(BF16)
                    start(hops[(sign, slot)])

        def reduce_second():
            for sign, out_buf, in_buf in sides:
                near = slice(0, 16) if sign == 1 else slice(16, 32)
                far = slice(16, 32) if sign == 1 else slice(0, 16)
                hops[(sign, 1)].wait_recv()
                hops[(sign, 0)].wait_recv()
                mine_ = own_block(chip(sign * 2)) + in_buf[j, 1, :, :].astype(F32)
                out_buf[j, 2, near, :] = (mine_[near, :] + in_buf[j, 0, near, :].astype(F32)).astype(BF16)
                out_buf[j, 2, far, :] = mine_[far, :].astype(BF16)
                start(hops[(sign, 2)])

        def reduce_third():
            for sign, out_buf, in_buf in sides:
                hops[(sign, 2)].wait_recv()
                out_buf[j, 3, :, :] = (own_block(chip(sign)) + in_buf[j, 2, :, :].astype(F32)).astype(BF16)
                start(hops[(sign, 3)])

        spread_steps, finish_ = gather(residual.at[j], deep)

        def own_sum():
            summed = own_block(z)
            for slot in (3,) if deep else (3, 2):
                for sign, out_buf, in_buf in sides:
                    hops[(sign, slot)].wait_recv()
                    summed = summed + in_buf[j, slot, :, :].astype(F32)
            spans = [slice(chunk_dp(j, s) * 128, chunk_dp(j, s) * 128 + 128) for s in range(N_X)]
            bias = jnp.concatenate([dec_bias[:, sp] for sp in spans], axis=1)
            rebuilt = summed + bias
            rebuilt_half = rebuilt.astype(BF16)
            for s, sp in enumerate(spans):
                rebuilt_out[:, sp] = rebuilt_half[:, s * 128:(s + 1) * 128]
            ins = jnp.concatenate([inputs[own, sp] for sp in spans], axis=1).astype(F32)
            residual[j, own, :] = (rebuilt - ins).astype(BF16)
            spread_steps[0]()

        steps = [reduce_first, reduce_second] + ([reduce_third] if deep else []) + [own_sum] + spread_steps[1:]
        at_time(begin, start_half)
        at_time(begin + 0.5, own_part)
        for step_at, fn in zip(times, steps):
            at_time(step_at, fn)
        return times[-1], finish_

    def pair_reduce(pick_ref, split, first_in, second_in, hop, me):
        a, b = (0, split), (split, split)
        far = lax.rem(me + 2, N_X)
        up, down = lax.rem(me + 1, N_X), lax.rem(me + 3, N_X)
        full = (0, 2 * split)
        far_up = remote(pick_ref(far, a), first_in.at[0], hop(1))
        far_down = remote(pick_ref(far, b), first_in.at[1], hop(-1))
        near_up = remote(pick_ref(up, full), second_in.at[0], hop(1))
        near_down = remote(pick_ref(down, full), second_in.at[1], hop(-1))

        def go():
            start(far_up)
            start(far_down)

        def combine():
            for copy, place_, part, ref, nxt in (
                (far_up, up, a, first_in.at[0], near_up),
                (far_down, down, b, first_in.at[1], near_down),
            ):
                copy.wait_recv()
                spot = pick_ref(place_, part)
                spot[...] = (spot[...].astype(F32) + ref[...].astype(F32)).astype(BF16)
                start(nxt)

        def total():
            near_up.wait_recv()
            near_down.wait_recv()
            spot = pick_ref(me, full)
            return spot[...].astype(F32) + second_in[0].astype(F32) + second_in[1].astype(F32)

        return go, combine, total

    def direct_reduce(pick_ref, rows, arrivals, hop, me):
        copies = [
            remote(pick_ref(lax.rem(me + k, N_X), (0, rows)), arrivals.at[i], hop(k))
            for i, k in enumerate((2, 1, 3))
        ]

        def go():
            for copy in copies:
                start(copy)

        def total():
            out = pick_ref(me, (0, rows))[...].astype(F32)
            for i in (1, 2, 0):
                copies[i].wait_recv()
                out = out + arrivals[i].astype(F32)
            return out

        return go, None, total

    def grad_stream(term, r1, r2, u, s1, s2, out, rows):
        half = rows // 2
        split = half // 2
        parts = []
        for j in range(CHUNKS):
            both = []
            for o in range(2):
                me = x if o == 0 else y
                hop = at_x if o == 0 else at_y

                def pick_ref(i, part, j=j, o=o):
                    s = i if o == 0 else lax.rem(j - i + N_X, N_X)
                    return term.at[j, s, pl.ds(o * half + part[0], part[1])]

                both.append(pair_reduce(pick_ref, split, r1.at[j, o], r2.at[j, o], hop, me))
            parts.append(both)
        tail = []
        for o in range(2):
            me = y if o == 0 else x
            hop = at_y if o == 0 else at_x

            def pick_ref(i, part, o=o):
                j = lax.rem(i + (x if o == 0 else y), N_X)
                return u.at[o, j, pl.ds(part[0], part[1])]

            if s1 is None:
                tail.append(direct_reduce(pick_ref, half, s2.at[o], hop, me))
            else:
                tail.append(pair_reduce(pick_ref, split, s1.at[o], s2.at[o], hop, me))

        def fold(j):
            def run():
                for o in range(2):
                    u[o, j] = parts[j][o][2]().astype(BF16)
            return run

        def go(j):
            for o in range(2):
                parts[j][o][0]()

        def combine(j):
            def run():
                for o in range(2):
                    parts[j][o][1]()
            return run

        def tail_go():
            for o in range(2):
                tail[o][0]()

        def tail_combine():
            for o in range(2):
                tail[o][1]()

        def tail_total():
            for o in range(2):
                out[o * half:(o + 1) * half, :] = tail[o][2]()

        return go, combine, fold, tail_go, tail_combine, tail_total

    dec_go, dec_combine, dec_fold, dec_tail_go, dec_tail_combine, dec_tail_total = grad_stream(
        dec_term, dec_r1, dec_r2, dec_u, dec_s1, dec_s2, dec_out, LAT
    )
    enc_go, enc_combine, enc_fold, enc_tail_go, _, enc_tail_total = grad_stream(
        enc_term, enc_r1, enc_r2, enc_u, None, enc_s, enc_out, 128
    )

    def dec_grad(j):
        def run():
            def tile_step(t, carry):
                at = pl.ds(pl.multiple_of(t * 256, 256), 256)
                term = GRAD_SCALE * dot(coded_t[at, :], residual[j])
                coef = dec_coef[at, :]
                for s in range(N_X):
                    sp = slice(s * 128, (s + 1) * 128)
                    dec_term[j, s, at, :] = (term[:, sp] + coef * dec_v[j, at, sp].astype(F32)).astype(BF16)
                return carry

            lax.fori_loop(0, LAT // 256, tile_step, 0)
            dec_go(j)
        return run

    def act_grad(j):
        def run():
            def tile_step(t, carry):
                at = pl.ds(pl.multiple_of(t * 256, 256), 256)
                part = dot_nt(residual[j], dec_v[j, at, :])
                if j == 0:
                    grad_act[:, at] = part
                elif j < CHUNKS - 1:
                    grad_act[:, at] = grad_act[:, at] + part
                else:
                    whole = GRAD_SCALE * (grad_act[:, at] + part) + norm_row[0:1, at]
                    grad_pre[:, at] = (whole * gate[:, at]).astype(BF16)
                return carry

            lax.fori_loop(0, LAT // 256, tile_step, 0)
        return run

    def enc_grad(j):
        def run():
            def tile_step(t, carry):
                at = pl.ds(pl.multiple_of(t * 256, 256), 256)
                term = dot(inputs_t[j], grad_pre[:, at]).astype(BF16)
                for s in range(N_X):
                    enc_term[j, s, :, at] = term[s * 128:(s + 1) * 128, :]
                return carry

            lax.fori_loop(0, LAT // 256, tile_step, 0)
            enc_go(j)
        return run

    WIRE = 4.2
    ready = 0.0
    for j in range(CHUNKS):
        t, all_in = latent_stream(j)
        ready = t
        at_time(ready, all_in)
        at_time(ready + 0.1, dec_grad(j))
        at_time(ready + 0.2, act_grad(j))
        at_time(ready + 4.5, dec_combine(j))
        at_time(ready + 9.0, dec_fold(j))
    dec_end = ready + 9.0
    enc_start = ready + 2.0
    for j in range(CHUNKS):
        t = enc_start + 1.0 * j
        at_time(t, enc_grad(j))
        at_time(t + 5.0 + (WIRE - 1.0) * j, enc_combine(j))
        at_time(t + 9.5 + (WIRE - 1.0) * j, enc_fold(j))
    enc_end = enc_start + 9.5 + WIRE * 3
    at_time(dec_end + 0.1, dec_tail_go)
    at_time(dec_end + 5.0, dec_tail_combine)
    at_time(dec_end + 12.0, dec_tail_total)
    at_time(enc_end + 0.1, enc_tail_go)
    at_time(enc_end + 8.0, enc_tail_total)

    for _, _, fn in sorted(events, key=lambda e: (e[0], e[1])):
        fn()
    for copy in sent:
        copy.wait_send()


def shards(
    queries, cache_keys, cache_values, positions, shuffle, enc_weight, enc_bias, dec_weight, dec_bias
):
    any_ = pl.BlockSpec(memory_space=pl.ANY)
    vmem = pl.BlockSpec(memory_space=pltpu.VMEM)
    scratch = [
        ((ROWS_DEV, WIDTH), BF16),
        ((CACHE, KV_HEADS * HEAD_DIM), BF16),
        ((CACHE, KV_HEADS * HEAD_DIM), BF16),
        ((WIDTH, LAT), BF16),
        ((CHUNKS, LAT, COLS), BF16),
        ((256, 256), BF16),
        ((256, 256), BF16),
        ((256, 256), BF16),
        ((128, 128), F32),
        ((128, 128), F32),
        ((16, 8, 128), F32),
        ((CHUNKS, GROUP, COLS), BF16),
        ((GROUP, WIDTH), BF16),
        ((256, WIDTH), BF16),
        ((CHUNKS, COLS, GROUP), BF16),
        ((GROUP, LAT), BF16),
        ((LAT, GROUP), BF16),
        ((GROUP, LAT), F32),
        ((8, LAT), F32),
        ((LAT, 128), F32),
        ((CHUNKS, 256, COLS), BF16),
        ((CHUNKS, 256, COLS), BF16),
        ((CHUNKS, 256, COLS), F32),
        ((CHUNKS, 4, ROWS_DEV, COLS), BF16),
        ((CHUNKS, 4, ROWS_DEV, COLS), BF16),
        ((CHUNKS, 4, ROWS_DEV, COLS), BF16),
        ((CHUNKS, 4, ROWS_DEV, COLS), BF16),
        ((CHUNKS, GROUP, COLS), BF16),
        ((GROUP, LAT), F32),
        ((GROUP, LAT), BF16),
        ((CHUNKS, 4, LAT, 128), BF16),
        ((CHUNKS, 4, 128, LAT), BF16),
        ((CHUNKS, 2, 2, 256, 128), BF16),
        ((CHUNKS, 2, 2, 512, 128), BF16),
        ((CHUNKS, 2, 2, 32, LAT), BF16),
        ((CHUNKS, 2, 2, 64, LAT), BF16),
        ((2, CHUNKS, 512, 128), BF16),
        ((2, CHUNKS, 64, LAT), BF16),
        ((2, 2, 256, 128), BF16),
        ((2, 2, 512, 128), BF16),
        ((2, 3, 64, LAT), BF16),
    ]
    return pl.pallas_call(
        kernel,
        out_shape=(
            pltpu.VMEM((ROWS_DEV, WIDTH), BF16),
            pltpu.VMEM((128, LAT), F32),
            pltpu.VMEM((LAT, 128), F32),
        ),
        in_specs=[any_, any_, any_, vmem, vmem, any_, vmem, any_, vmem],
        out_specs=(vmem, vmem, vmem),
        scratch_shapes=[pltpu.VMEM(shape, dtype) for shape, dtype in scratch]
        + [
            pltpu.SemaphoreType.DMA((N_SEMS,)),
            pltpu.SemaphoreType.DMA((N_SEMS,)),
            pltpu.SemaphoreType.DMA((20,)),
        ],
        compiler_params=pltpu.CompilerParams(
            collective_id=0, has_side_effects=True, vmem_limit_bytes=64000000
        ),
    )(
        queries, cache_keys, cache_values, positions.reshape(1, -1), shuffle.reshape(1, -1),
        enc_weight, enc_bias.reshape(1, -1), dec_weight, dec_bias.reshape(1, -1),
    )


def solution(mesh):
    in_specs = (
        P(("dp", "latent"), None),
        P(("dp", "latent"), None, None),
        P(("dp", "latent"), None, None),
        P(("dp", "latent")),
        P(("dp", "latent")),
        P(None, "latent"),
        P("latent"),
        P("latent", None),
        P(),
    )
    out_specs = (P(("dp", "latent"), None), P("dp", "latent"), P("latent", "dp"))
    return jax.shard_map(shards, mesh=mesh, in_specs=in_specs, out_specs=out_specs, check_vma=False)
```
